512 devices in a mesh: pat: 32 (over x, z_lo), ori: 16 (over z_hi, y, core).
Axes of the slice: x: 4, y: 4, z: 16 (z_hi: 2, z_lo: 8; z = z_hi * 8 + z_lo), core: 2. Of those that a mesh axis runs over, the one named last changes fastest.
Arguments:
- patterns: bfloat16 [12288, 4096], P('pat'), may hold values from 0 to 240, as said below
- mask: int32 [12288], P('pat'), may hold values 0 or 1
- model: float32 [1024, 64], replicated, may hold values from -0.09375 to 0.09375
- wigner: bfloat16 [2048, 1024], P('ori'), may hold values from -6 to 6
Outputs:
- harmonics: float32 [1024, 64], P('ori', 'pat')
The draws below stay inside these ranges and needn't reach their ends.
Inputs may be any that keep to these rules, and one draw needn't show every extreme that they name: `patterns`: photon counts scaled by each pattern's fluence and each pixel's response.
All inputs are finite; a program needn't handle non-finite values. No bound on the sum of `mask` on one device may be relied on, other than what follows from the above.
Results may differ from the reference program's by a relative error of at most 0.0075.
Values may be sent and summed in bfloat16 or wider, within the bound.
A program may use at most 64 MiB of HBM per device.

```python
import math
import jax
import jax.numpy as jnp
from jax import lax

RADII = 64
ANGLES = 64
DEG = 16
ORD = 64
PIX = 4096
HARM = 1024
PATTERNS = 12288
ORIENTS = 2048


def draw_patterns(key, part):
    row_key, column_key, photon_key = jax.random.split(key, 3)
    column_scale = jnp.exp(jax.random.uniform(column_key, (1, PIX), minval=math.log(0.3), maxval=math.log(3.0)))
    row_scale = jnp.exp(jax.random.uniform(row_key, (PATTERNS, 1), minval=0.0, maxval=math.log(10.0)))
    photon_base = jax.random.uniform(photon_key, (PATTERNS, PIX), minval=0.0, maxval=2.0)
    return (row_scale * column_scale * photon_base).astype(jnp.bfloat16)


def touch_ends(result, rng, smallest, high):
    longest = result.shape.index(max(result.shape))
    spots = []
    for shift in (0, 1):
        where = [jax.random.randint(jax.random.fold_in(rng, axis), (), 0, length) for axis, length in enumerate(result.shape)]
        where[longest] = (where[longest] + shift) % result.shape[longest]
        spots.append(tuple(where))
    return result.at[spots[0]].set(smallest).at[spots[1]].set(high)


def shard_levels(own_key, shape, cuts, least, largest):
    level = 1.0
    for dim, parts in cuts:
        steps = jax.random.uniform(jax.random.fold_in(jax.random.fold_in(own_key, 6), dim), (parts,), jnp.float32, least / len(cuts), largest / len(cuts))
        level = level * jnp.repeat(jnp.exp(steps), shape[dim] // parts).reshape((-1,) + (1,) * (len(shape) - 1 - dim))
    return level


def normal_values(own_key, extent, scale, limit, shards=(), held_as=jnp.bfloat16):
    drawn = scale * jax.random.normal(own_key, extent, jnp.float32)
    if shards:
        drawn = drawn * shard_levels(own_key, extent, shards, -0.22, 0.18)
    return jnp.clip(drawn, -limit, limit).astype(held_as)


def setup_inputs(seed: int = 0) -> dict:
    splits = jax.random.split(jax.random.key(seed), 5)
    patterns = draw_patterns(jax.random.fold_in(splits[4], 71), 0)
    mask = touch_ends((jax.random.randint(splits[1], (PATTERNS,), 0, 4) < 3).astype(jnp.int32), jax.random.fold_in(splits[1], 1), 0, 1)
    model = normal_values(splits[2], (HARM, RADII), 0.015, 0.09375, (), jnp.float32)
    wigner = normal_values(splits[3], (ORIENTS, HARM), 1.0, 6.0, ((0, 16),))
    return dict(patterns=patterns, mask=mask, model=model, wigner=wigner)


temper = 0.05
background = 0.1

def order_table():
    orders = jnp.arange(ORD, dtype=jnp.int32)[:, None]
    angles = jnp.arange(ANGLES, dtype=jnp.int32)[None, :]
    half_way = ANGLES // 2
    phase_cos = 2.0 * math.pi / ANGLES * (orders * angles).astype(jnp.float32)
    phase_sin = 2.0 * math.pi / ANGLES * ((orders - half_way) * angles).astype(jnp.float32)
    return jnp.where(orders <= half_way, jnp.cos(phase_cos), jnp.sin(phase_sin))

def reference(patterns, mask, model, wigner):
    highest = lax.Precision.HIGHEST
    synthesis = order_table()
    harmonic_rows = wigner.astype(jnp.float32).reshape(ORIENTS, ORD, DEG)
    cycle_model = jnp.einsum('rkd,kdb->rkb', harmonic_rows, model.reshape(ORD, DEG, RADII), precision=highest)
    log_slices = (background + jnp.einsum('rkb,ka->rba', cycle_model, synthesis, precision=highest)).reshape(ORIENTS, PIX).astype(jnp.bfloat16)
    intensity = lax.optimization_barrier(jnp.sum(jnp.exp(log_slices.astype(jnp.float32)), axis=1))
    products = jnp.dot(patterns.astype(jnp.float32), log_slices.astype(jnp.float32).T, precision=highest)
    scores = temper * (products - intensity[None, :])
    row_peak = lax.optimization_barrier(jnp.max(scores, axis=1, keepdims=True))
    exponent = jnp.exp(scores - row_peak)
    weights = (exponent / lax.optimization_barrier(jnp.sum(exponent, axis=1, keepdims=True)) * mask.astype(jnp.float32)[:, None]).astype(jnp.bfloat16)
    occupancy = lax.optimization_barrier(jnp.sum(weights.astype(jnp.float32), axis=0))
    weighted = jnp.dot(weights.astype(jnp.float32).T, patterns.astype(jnp.float32), precision=highest)
    slices = weighted / (occupancy + 1.0)[:, None]
    cycle_data = 2.0 / ANGLES * jnp.einsum('rba,ka->rkb', slices.reshape(ORIENTS, RADII, ANGLES), synthesis, precision=highest)
    harmonics = jnp.einsum('rkd,rkb->kdb', harmonic_rows, cycle_data, precision=highest) / math.sqrt(ORIENTS)
    return harmonics.reshape(HARM, RADII)
```

```python
import math

import jax
import jax.numpy as jnp
import numpy as np
from jax import lax
from jax.experimental import pallas as pl
from jax.experimental.pallas import tpu as pltpu
from jax.sharding import PartitionSpec as P

RADII = 64
ANGLES = 64
DEG = 16
ORD = 64
PIX = 4096
HARM = 1024
PATTERNS = 12288
ORIENTS = 2048

TEMPER = 0.05
BACKGROUND = 0.1

NX, NZ = 4, 8
NH, NQ = 2, 8
PLANE = NX * NQ
RING = NH * NZ
OWN_P = PATTERNS // (NX * NZ)
OWN_R = ORIENTS // (NH * NQ)
PT = OWN_P // 128
BLK = 4 * ANGLES
NBLK = PIX // BLK

F32 = jnp.float32
BF16 = jnp.bfloat16
MESH = pl.DeviceIdType.MESH


def order_table():
    orders = np.arange(ORD)[:, None]
    angles = np.arange(ANGLES)[None, :]
    half = ANGLES // 2
    step = 2.0 * math.pi / ANGLES
    cos = np.cos(step * ((orders * angles) % ANGLES))
    sin = np.sin(step * (((orders - half) * angles) % ANGLES))
    return np.where(orders <= half, cos, sin).astype(np.float32)


def two_terms(block):
    full = np.kron(np.eye(4, dtype=np.float32), block.astype(np.float32))
    high = full.astype(BF16)
    low = (full - high.astype(np.float32)).astype(BF16)
    return np.stack([high, low])


def split(value):
    high = value.astype(BF16)
    low = (value - high.astype(F32)).astype(BF16)
    return high, low


def dot(a, b):
    return jnp.dot(a, b, preferred_element_type=F32)


def apply_table(table_ref, value):
    high, low = split(value)
    both = dot(table_ref[0], jnp.concatenate([high, low], axis=1))
    return both[:, :OWN_R] + both[:, OWN_R:] + dot(table_ref[1], high)


def kernel(
    pat_hbm, mask_ref, model_ref, wig_ref, syn_ref, fwd_ref, out_ref,
    pat, pat_t, cyc, logs, score, wig_p, wt, ordt,
    stat, b1, pair, b2, occ1, c1, occ2, c2, harm, e1, zsum, zsend, e2,
    in_sem, b1_s, b1_r, b2_s, b2_r, c1_s, c1_r, c2_s, c2_r, e1_s, e1_r, e2_s, e2_r,
):
    p_id = lax.axis_index("pat")
    o_id = lax.axis_index("ori")
    x, zl = lax.div(p_id, NZ), lax.rem(p_id, NZ)
    zh, q = lax.div(o_id, NQ), lax.rem(o_id, NQ)
    z = zh * NZ + zl

    def plane_peer(dx, dq):
        return (lax.rem(x + dx, NX) * NZ + zl, zh * NQ + lax.rem(q + dq, NQ))

    def ring_peer(dz):
        far = lax.rem(z + dz, RING)
        return (x * NZ + lax.rem(far, NZ), lax.div(far, NZ) * NQ + q)

    def low_peer(dz):
        return (x * NZ + lax.rem(zl + dz, NZ), o_id)

    def send(src, dst, ssem, rsem, peer):
        pltpu.make_async_remote_copy(
            src_ref=src, dst_ref=dst, send_sem=ssem, recv_sem=rsem,
            device_id=peer, device_id_type=MESH,
        ).start()

    def finish(buf, ssem, rsem, peer):
        copy = pltpu.make_async_remote_copy(
            src_ref=buf, dst_ref=buf, send_sem=ssem, recv_sem=rsem,
            device_id=peer, device_id_type=MESH,
        )
        copy.wait_send()
        copy.wait_recv()

    load = pltpu.make_async_copy(pat_hbm, pat, in_sem)
    load.start()

    barrier = pltpu.get_barrier_semaphore()

    @pl.loop(1, PLANE)
    def _(j):
        pl.semaphore_signal(
            barrier, inc=1, device_id=plane_peer(lax.div(j, NQ), lax.rem(j, NQ)),
            device_id_type=MESH,
        )

    @pl.loop(1, RING)
    def _(j):
        pl.semaphore_signal(barrier, inc=1, device_id=ring_peer(j), device_id_type=MESH)

    row = lax.broadcasted_iota(jnp.int32, (8, 128), 0)
    lane = lax.broadcasted_iota(jnp.int32, (8, 128), 1)
    diag = jnp.where(lax.div(lane, DEG) == row, 1.0, 0.0).astype(F32)

    @pl.loop(0, ORD // 8)
    def _(g):
        cols = pl.ds(pl.multiple_of(g * 128, 128), 128)
        m = model_ref[:, cols]
        high = m.astype(BF16).astype(F32)
        low = m - high
        left = jnp.concatenate(
            [
                (high[:, None, :] * diag[None]).reshape(512, 128).astype(BF16),
                (low[:, None, :] * diag[None]).reshape(512, 128).astype(BF16),
            ],
            axis=1,
        )
        w = wig_ref[:, cols]
        out = lax.dot_general(
            left, jnp.concatenate([w, w], axis=1), (((1,), (1,)), ((), ())),
            preferred_element_type=F32,
        )
        cyc[:, pl.ds(pl.multiple_of(g * 8, 8), 8), :] = out.reshape(RADII, 8, OWN_R)

    def expand(j, total):
        c = cyc[pl.ds(j * 4, 4)].reshape(BLK, OWN_R)
        value = (BACKGROUND + apply_table(syn_ref, c)).astype(BF16)
        logs[pl.ds(pl.multiple_of(j * BLK, BLK), BLK), :] = value
        e = jnp.exp(value.astype(F32))
        return total + jnp.sum(e.reshape(BLK // 8, 8, OWN_R), axis=0)

    total = lax.fori_loop(0, NBLK, expand, jnp.zeros((8, OWN_R), F32))
    intensity = jnp.sum(total, axis=0, keepdims=True)

    load.wait()
    prod = dot(pat[...], logs[...])
    scaled = TEMPER * (prod - intensity)
    for t in range(PT):
        score[t] = scaled[t * 128:(t + 1) * 128, :].T
    peaks, masses = [], []
    for t in range(PT):
        s = score[t]
        m = jnp.max(s, axis=0, keepdims=True)
        peaks.append(m)
        masses.append(jnp.sum(jnp.exp(s - m), axis=0, keepdims=True))
    blank = jnp.zeros((8 - 2 * PT, 128), F32)
    stat[...] = jnp.concatenate(peaks + masses + [blank], axis=0)

    pl.semaphore_wait(barrier, PLANE - 1 + RING - 1)

    @pl.loop(1, NQ)
    def _(j):
        send(stat, b1.at[j - 1], b1_s, b1_r, plane_peer(0, j))

    low_half = lax.broadcasted_iota(jnp.int32, (OWN_R, 128), 1) < 64
    for t in range(NQ // 2):
        a = wig_ref[:, t * 128:(t + 1) * 128].astype(F32)
        b = wig_ref[:, 512 + t * 128:512 + (t + 1) * 128].astype(F32)
        wig_p[2 * t] = jnp.where(low_half, a, pltpu.roll(b, 64, 1)).astype(BF16)
        wig_p[2 * t + 1] = jnp.where(low_half, pltpu.roll(a, 64, 1), b).astype(BF16)

    finish(b1, b1_s, b1_r, plane_peer(0, 1))
    peak = stat[0:PT, :]
    for j in range(NQ - 1):
        peak = jnp.maximum(peak, b1[j, 0:PT, :])
    mass = stat[PT:2 * PT, :] * jnp.exp(stat[0:PT, :] - peak)
    for j in range(NQ - 1):
        mass = mass + b1[j, PT:2 * PT, :] * jnp.exp(b1[j, 0:PT, :] - peak)
    pair[...] = jnp.concatenate([peak, mass, blank], axis=0)
    send(pair, b2, b2_s, b2_r, ring_peer(NZ))

    @pl.loop(0, PIX // 128)
    def _(j):
        span = pl.ds(pl.multiple_of(j * 128, 128), 128)
        pat_t[span, :] = pat[:, span].T

    finish(b2, b2_s, b2_r, ring_peer(NZ))
    far_peak = b2[0:PT, :]
    top = jnp.maximum(peak, far_peak)
    mass = mass * jnp.exp(peak - top) + b2[PT:2 * PT, :] * jnp.exp(far_peak - top)
    part = jnp.zeros((8, OWN_R), F32)
    for t in range(PT):
        factor = mask_ref[:, t * 128:(t + 1) * 128].astype(F32) / mass[t:t + 1, :]
        w = (jnp.exp(score[t] - top[t:t + 1, :]) * factor).T.astype(BF16)
        wt[t * 128:(t + 1) * 128, :] = w
        part = part + jnp.sum(w.astype(F32).reshape(16, 8, OWN_R), axis=0)
    occ1[...] = jnp.sum(part, axis=0, keepdims=True)

    @pl.loop(1, NX)
    def _(j):
        send(occ1, c1.at[j - 1], c1_s, c1_r, plane_peer(j, 0))

    def compress(j, carry):
        rows = pl.ds(pl.multiple_of(j * BLK, BLK), BLK)
        ordt[rows, :] = apply_table(fwd_ref, dot(pat_t[rows, :], wt[...]))
        return carry

    lax.fori_loop(0, NBLK // 2, compress, 0)
    finish(c1, c1_s, c1_r, plane_peer(1, 0))
    occ = occ1[...]
    for j in range(NX - 1):
        occ = occ + c1[j]
    occ2[...] = occ

    @pl.loop(1, NZ)
    def _(j):
        send(occ2, c2.at[j - 1], c2_s, c2_r, low_peer(j))

    lax.fori_loop(NBLK // 2, NBLK, compress, 0)
    finish(c2, c2_s, c2_r, low_peer(1))
    for j in range(NZ - 1):
        occ = occ + c2[j]
    inv = (1.0 / math.sqrt(ORIENTS)) / (occ + 1.0)

    slot = lax.div(lax.broadcasted_iota(jnp.int32, (RADII, 128), 1), DEG)

    def project(i, carry):
        g = lax.rem(q + i, NQ)
        lefts = []
        for kk in range(8):
            k = (kk // 4) * (ORD // 2) + g * 4 + kk % 4
            o = ordt[pl.ds(k, RADII, stride=ORD), :] * inv
            high, low = split(o)
            lefts.append(jnp.concatenate([high, low], axis=1))
        w = wig_p[g]
        out = dot(jnp.concatenate(lefts, axis=0), jnp.concatenate([w, w], axis=0))
        acc = jnp.zeros((RADII, 128), F32)
        for kk in range(8):
            acc = jnp.where(slot == kk, out[kk * RADII:(kk + 1) * RADII, :], acc)
        harm[g] = acc.reshape(NX, 16, 128)

        for dx in range(NX):
            far = lax.rem(x + dx, NX)
            n = dx * NQ + i

            @pl.when(n > 0)
            def _():
                send(
                    harm.at[g, far], e1.at[jnp.maximum(n - 1, 0)], e1_s, e1_r,
                    plane_peer(dx, i),
                )
        return carry

    lax.fori_loop(0, NQ, project, 0)
    finish(e1, e1_s, e1_r, plane_peer(1, 0))
    tot = harm[q, x]
    for j in range(PLANE - 1):
        tot = tot + e1[j]
    zsum[...] = tot
    even = zsum[pl.ds(0, 8, stride=2), :]
    odd = zsum[pl.ds(1, 8, stride=2), :]
    first = lane < 64
    rows = jnp.concatenate(
        [
            jnp.where(first, even, pltpu.roll(odd, 64, 1)),
            jnp.where(first, pltpu.roll(even, 64, 1), odd),
        ],
        axis=0,
    )
    for j in range(RING):
        zsend[j] = rows[j:j + 1, :]

    @pl.loop(1, RING)
    def _(j):
        send(zsend.at[lax.rem(z + j, RING)], e2.at[j - 1], e2_s, e2_r, ring_peer(j))

    finish(e2, e2_s, e2_r, ring_peer(1))
    fin = zsend[z]
    for j in range(RING - 1):
        fin = fin + e2[j]
    out_ref[0:1, :] = fin[:, :64]
    out_ref[1:2, :] = fin[:, 64:]


def local(patterns, mask, model, wigner):
    table = order_table()
    syn = jnp.asarray(two_terms(table.T))
    fwd = jnp.asarray(two_terms(table * (2.0 / ANGLES)))
    vmem = pl.BlockSpec(memory_space=pltpu.VMEM)
    dma = pltpu.SemaphoreType.DMA
    out = pl.pallas_call(
        kernel,
        out_shape=jax.ShapeDtypeStruct((2, 64), F32),
        in_specs=[pl.BlockSpec(memory_space=pl.ANY)] + [vmem] * 5,
        out_specs=vmem,
        scratch_shapes=[
            pltpu.VMEM((OWN_P, PIX), BF16),
            pltpu.VMEM((PIX, OWN_P), BF16),
            pltpu.VMEM((RADII, ORD, OWN_R), F32),
            pltpu.VMEM((PIX, OWN_R), BF16),
            pltpu.VMEM((PT, OWN_R, 128), F32),
            pltpu.VMEM((NQ, OWN_R, 128), BF16),
            pltpu.VMEM((OWN_P, OWN_R), BF16),
            pltpu.VMEM((PIX, OWN_R), F32),
            pltpu.VMEM((8, 128), F32),
            pltpu.VMEM((NQ - 1, 8, 128), F32),
            pltpu.VMEM((8, 128), F32),
            pltpu.VMEM((8, 128), F32),
            pltpu.VMEM((1, 128), F32),
            pltpu.VMEM((NX - 1, 1, 128), F32),
            pltpu.VMEM((1, 128), F32),
            pltpu.VMEM((NZ - 1, 1, 128), F32),
            pltpu.VMEM((NQ, NX, 16, 128), F32),
            pltpu.VMEM((PLANE - 1, 16, 128), F32),
            pltpu.VMEM((16, 128), F32),
            pltpu.VMEM((RING, 1, 128), F32),
            pltpu.VMEM((RING - 1, 1, 128), F32),
        ]
        + [dma(())] * 13,
        compiler_params=pltpu.CompilerParams(collective_id=0, has_side_effects=True),
        name="recover",
    )(patterns, mask.reshape(1, OWN_P), model.T, wigner, syn, fwd)
    return out.T


def solution(mesh):
    return jax.shard_map(
        local,
        mesh=mesh,
        in_specs=(P("pat", None), P("pat"), P(), P("ori", None)),
        out_specs=P("ori", "pat"),
        check_vma=False,
    )
```

```python
import math

import jax
import jax.numpy as jnp
import numpy as np
from jax import lax
from jax.experimental import pallas as pl
from jax.experimental.pallas import tpu as pltpu
from jax.sharding import PartitionSpec as P

RADII = 64
ANGLES = 64
DEG = 16
ORD = 64
PIX = 4096
HARM = 1024
PATTERNS = 12288
ORIENTS = 2048

TEMPER = 0.05
BACKGROUND = 0.1

NX, NZ = 4, 8
NH, NQ = 2, 8
PLANE = NX * NQ
RING = NH * NZ
OWN_P = PATTERNS // (NX * NZ)
OWN_R = ORIENTS // (NH * NQ)
PT = OWN_P // 128
BLK = 4 * ANGLES
NBLK = PIX // BLK

F32 = jnp.float32
BF16 = jnp.bfloat16
MESH = pl.DeviceIdType.MESH


def order_table():
    orders = np.arange(ORD)[:, None]
    angles = np.arange(ANGLES)[None, :]
    half = ANGLES // 2
    step = 2.0 * math.pi / ANGLES
    cos = np.cos(step * ((orders * angles) % ANGLES))
    sin = np.sin(step * (((orders - half) * angles) % ANGLES))
    return np.where(orders <= half, cos, sin).astype(np.float32)


def two_terms(full):
    high = full.astype(BF16)
    low = (full - high.astype(np.float32)).astype(BF16)
    return np.stack([high, low])


def tables():
    table = order_table()
    eye = np.eye(4, dtype=np.float32)
    syn = np.einsum("ka,bc->bakc", table, eye).reshape(BLK, BLK)
    fwd = np.einsum("ka,bc->kbca", table * np.float32(2.0 / ANGLES), eye)
    swap = fwd[np.arange(ORD) ^ 1]
    return (
        two_terms(syn),
        np.stack([two_terms(fwd.reshape(BLK, BLK)), two_terms(swap.reshape(BLK, BLK))]),
    )


def split(value):
    high = value.astype(BF16)
    low = (value - high.astype(F32)).astype(BF16)
    return high, low


def dot(a, b):
    return jnp.dot(a, b, preferred_element_type=F32)


def apply_table(table_ref, value):
    high, low = split(value)
    both = dot(table_ref[0], jnp.concatenate([high, low], axis=1))
    return both[:, :OWN_R] + both[:, OWN_R:] + dot(table_ref[1], high)


def far_first(n):
    return sorted(range(1, n), key=lambda j: -min(j, n - j))


def kernel(
    pat_hbm, mask_hbm, model_hbm, wig_hbm, syn_hbm, fwd_hbm, out_ref,
    pat, mask, model, wig, syn, fwd,
    pat_t, cyc, logs, score, wig_p, wt, ordt,
    stat, b1, pair, b2, occ1, c1, occ2, c2, harm, e1, zsum, zsend, e2,
    pat_sem, mask_sem, model_sem, wig_sem, syn_sem, fwd_sem,
    b1_s, b1_r, b2_s, b2_r, c1_s, c1_r, c2_s, c2_r, e1_s, e1_r, e2_s, e2_r,
):
    p_id = lax.axis_index("pat")
    o_id = lax.axis_index("ori")
    x, zl = lax.div(p_id, NZ), lax.rem(p_id, NZ)
    zh, q = lax.div(o_id, NQ), lax.rem(o_id, NQ)
    z = zh * NZ + zl

    def plane_peer(dx, dq):
        return (lax.rem(x + dx, NX) * NZ + zl, zh * NQ + lax.rem(q + dq, NQ))

    def ring_peer(dz):
        far = lax.rem(z + dz, RING)
        return (x * NZ + lax.rem(far, NZ), lax.div(far, NZ) * NQ + q)

    def low_peer(dz):
        return (x * NZ + lax.rem(zl + dz, NZ), o_id)

    def greet(peer):
        pl.semaphore_signal(barrier, inc=1, device_id=peer, device_id_type=MESH)

    def send(src, dst, ssem, rsem, peer):
        pltpu.make_async_remote_copy(
            src_ref=src, dst_ref=dst, send_sem=ssem, recv_sem=rsem,
            device_id=peer, device_id_type=MESH,
        ).start()

    def finish(buf, ssem, rsem, peer):
        copy = pltpu.make_async_remote_copy(
            src_ref=buf, dst_ref=buf, send_sem=ssem, recv_sem=rsem,
            device_id=peer, device_id_type=MESH,
        )
        copy.wait_send()
        copy.wait_recv()

    loads = [
        pltpu.make_async_copy(*refs)
        for refs in (
            (model_hbm, model, model_sem), (wig_hbm, wig, wig_sem), (syn_hbm, syn, syn_sem),
            (pat_hbm, pat, pat_sem), (fwd_hbm, fwd, fwd_sem), (mask_hbm, mask, mask_sem),
        )
    ]
    model_in, wig_in, syn_in, pat_in, fwd_in, mask_in = loads
    for load in loads:
        load.start()

    barrier = pltpu.get_barrier_semaphore()
    greet(ring_peer(NZ))
    for j in far_first(NZ):
        greet(low_peer(j))
    for j in far_first(NX):
        greet(plane_peer(j, 0))
    for j in far_first(NQ):
        greet(plane_peer(0, j))

    row = lax.broadcasted_iota(jnp.int32, (16, 128), 0)
    lane = lax.broadcasted_iota(jnp.int32, (16, 128), 1)
    own = [
        jnp.where(lax.div(lane, DEG) == lax.div(row, 4) + n, 1.0, 0.0).astype(BF16)
        for n in (0, 4)
    ]
    upper = lax.broadcasted_iota(jnp.int32, (1, 8, 128), 1) < 4
    model_in.wait()
    wig_in.wait()

    def spread(value):
        tile = value.reshape(RADII // 8, 8, 128)
        other = pltpu.roll(tile, 4, 1)
        one = jnp.where(upper, tile, other)
        two = jnp.where(upper, other, tile)
        rows = []
        for i in range(RADII // 8):
            for half in (one[i], two[i]):
                packed = jnp.concatenate([half, half], axis=0).astype(BF16)
                rows += [packed * own[0], packed * own[1]]
        return jnp.concatenate(rows, axis=0)

    def gather_cycles(g):
        cols = pl.ds(pl.multiple_of(g * 128, 128), 128)
        m = model[:, cols]
        high = m.astype(BF16).astype(F32)
        left = jnp.concatenate([spread(high), spread(m - high)], axis=1)
        w = wig[:, cols]
        out = lax.dot_general(
            left, jnp.concatenate([w, w], axis=1), (((1,), (1,)), ((), ())),
            preferred_element_type=F32,
        )
        cyc[:, pl.ds(pl.multiple_of(g * 32, 32), 32), :] = out.reshape(NBLK, 32, OWN_R)

    @pl.loop(0, ORD // 16)
    def _(g):
        gather_cycles(2 * g)
        gather_cycles(2 * g + 1)

    syn_in.wait()

    def expand(j, total):
        value = (BACKGROUND + apply_table(syn, cyc[j])).astype(BF16)
        logs[pl.ds(pl.multiple_of(j * BLK, BLK), BLK), :] = value
        e = jnp.exp(value.astype(F32))
        return total + jnp.sum(e.reshape(BLK // 8, 8, OWN_R), axis=0)

    def expand_four(j, total):
        for n in range(4):
            total = expand(4 * j + n, total)
        return total

    total = lax.fori_loop(0, NBLK // 4, expand_four, jnp.zeros((8, OWN_R), F32))
    intensity = jnp.sum(total, axis=0, keepdims=True)

    pat_in.wait()
    scaled = TEMPER * (dot(pat[...], logs[...]) - intensity)
    for t in range(PT):
        score[t] = scaled[t * 128:(t + 1) * 128, :].T
    peaks, masses = [], []
    for t in range(PT):
        s = score[t]
        m = jnp.max(s, axis=0, keepdims=True)
        peaks.append(m)
        masses.append(jnp.sum(jnp.exp(s - m), axis=0, keepdims=True))
    blank = jnp.zeros((8 - 2 * PT, 128), F32)
    stat[...] = jnp.concatenate(peaks + masses + [blank], axis=0)

    pl.semaphore_wait(barrier, 1 + NZ - 1 + NX - 1 + NQ - 1)

    for j in far_first(NQ):
        send(stat, b1.at[j - 1], b1_s, b1_r, plane_peer(0, j))

    fwd_in.wait()
    mask_in.wait()
    low_half = lax.broadcasted_iota(jnp.int32, (OWN_R, 128), 1) < 64
    for t in range(NQ // 2):
        a = wig[:, t * 128:(t + 1) * 128].astype(F32)
        b = wig[:, 512 + t * 128:512 + (t + 1) * 128].astype(F32)
        wig_p[2 * t] = jnp.where(low_half, a, pltpu.roll(b, 64, 1)).astype(BF16)
        wig_p[2 * t + 1] = jnp.where(low_half, pltpu.roll(a, 64, 1), b).astype(BF16)

    finish(b1, b1_s, b1_r, plane_peer(0, 1))
    peak = stat[0:PT, :]
    for j in range(NQ - 1):
        peak = jnp.maximum(peak, b1[j, 0:PT, :])
    mass = stat[PT:2 * PT, :] * jnp.exp(stat[0:PT, :] - peak)
    for j in range(NQ - 1):
        mass = mass + b1[j, PT:2 * PT, :] * jnp.exp(b1[j, 0:PT, :] - peak)
    pair[...] = jnp.concatenate([peak, mass, blank], axis=0)
    send(pair, b2, b2_s, b2_r, ring_peer(NZ))

    @pl.loop(0, PIX // 128)
    def _(j):
        span = pl.ds(pl.multiple_of(j * 128, 128), 128)
        pat_t[span, :] = pat[:, span].T

    finish(b2, b2_s, b2_r, ring_peer(NZ))
    far_peak = b2[0:PT, :]
    top = jnp.maximum(peak, far_peak)
    mass = mass * jnp.exp(peak - top) + b2[PT:2 * PT, :] * jnp.exp(far_peak - top)
    part = jnp.zeros((8, OWN_R), F32)
    for t in range(PT):
        counts = mask[t * 128:(t + 1) * 128].astype(F32).reshape(1, 128)
        factor = counts / mass[t:t + 1, :]
        w = (jnp.exp(score[t] - top[t:t + 1, :]) * factor).T.astype(BF16)
        wt[t * 128:(t + 1) * 128, :] = w
        part = part + jnp.sum(w.astype(F32).reshape(16, 8, OWN_R), axis=0)
    occ1[...] = jnp.sum(part, axis=0, keepdims=True)

    for j in far_first(NX):
        send(occ1, c1.at[j - 1], c1_s, c1_r, plane_peer(j, 0))

    def compress(i, carry):
        parts = []
        for n in range(2):
            rows = pl.ds(pl.multiple_of((2 * i + n) * BLK, BLK), BLK)
            parts.append(
                apply_table(fwd.at[n], dot(pat_t[rows, :], wt[...])).reshape(ORD // 2, 8, OWN_R)
            )
        cols = pl.ds(pl.multiple_of(i * 8, 8), 8)
        ordt[:, 0, cols, :] = jnp.where(upper, parts[0], parts[1])
        ordt[:, 1, cols, :] = jnp.where(upper, parts[1], parts[0])
        return carry

    lax.fori_loop(0, 2, compress, 0)
    finish(c1, c1_s, c1_r, plane_peer(1, 0))
    occ = occ1[...]
    for j in range(NX - 1):
        occ = occ + c1[j]
    occ2[...] = occ

    for j in far_first(NZ):
        send(occ2, c2.at[j - 1], c2_s, c2_r, low_peer(j))

    lax.fori_loop(2, NBLK // 2, compress, 0)
    finish(c2, c2_s, c2_r, low_peer(1))
    for j in range(NZ - 1):
        occ = occ + c2[j]
    inv = (1.0 / math.sqrt(ORIENTS)) / (occ + 1.0)

    slot = lax.div(lax.broadcasted_iota(jnp.int32, (RADII, 128), 1), DEG)

    def project(i):
        g = lax.rem(q + i, NQ)
        lefts = []
        for kk in range(8):
            o = ordt[(kk // 4) * (ORD // 4) + g * 2 + (kk % 4) // 2, kk % 2] * inv
            high, low = split(o)
            lefts.append(jnp.concatenate([high, low], axis=1))
        w = wig_p[g]
        out = dot(jnp.concatenate(lefts, axis=0), jnp.concatenate([w, w], axis=0))
        acc = [jnp.zeros((RADII, 128), F32)] * 2
        for kk in range(8):
            acc[kk % 2] = jnp.where(slot == kk, out[kk * RADII:(kk + 1) * RADII, :], acc[kk % 2])
        odd = pltpu.roll(acc[1].reshape(RADII // 8, 8, 128), 4, 1).reshape(RADII, 128)
        harm[g] = (acc[0] + odd).astype(BF16).reshape(NX, 16, 128)
        for dx in (2, 1, 3, 0):
            if dx or i:
                send(
                    harm.at[g, lax.rem(x + dx, NX)], e1.at[dx * NQ + i - 1], e1_s, e1_r,
                    plane_peer(dx, i),
                )

    for i in far_first(NQ) + [0]:
        project(i)
    finish(e1, e1_s, e1_r, plane_peer(1, 0))
    tot = harm[q, x].astype(F32)
    for j in range(PLANE - 1):
        tot = tot + e1[j].astype(F32)
    zsum[...] = tot
    even = zsum[pl.ds(0, 8, stride=2), :]
    odd = zsum[pl.ds(1, 8, stride=2), :]
    first = lane[:8] < 64
    rows = jnp.concatenate(
        [
            jnp.where(first, even, pltpu.roll(odd, 64, 1)),
            jnp.where(first, pltpu.roll(even, 64, 1), odd),
        ],
        axis=0,
    )
    for j in range(RING):
        zsend[j] = rows[j:j + 1, :]
    for j in far_first(RING):
        send(zsend.at[lax.rem(z + j, RING)], e2.at[j - 1], e2_s, e2_r, ring_peer(j))
    finish(e2, e2_s, e2_r, ring_peer(1))
    fin = zsend[z]
    for j in range(RING - 1):
        fin = fin + e2[j]
    out_ref[0:1, :] = fin[:, :64]
    out_ref[1:2, :] = fin[:, 64:]


def local(patterns, mask, model, wigner):
    syn, fwd = tables()
    hbm = pl.BlockSpec(memory_space=pl.ANY)
    dma = pltpu.SemaphoreType.DMA
    out = pl.pallas_call(
        kernel,
        out_shape=jax.ShapeDtypeStruct((2, 64), F32),
        in_specs=[hbm] * 6,
        out_specs=pl.BlockSpec(memory_space=pltpu.VMEM),
        scratch_shapes=[
            pltpu.VMEM((OWN_P, PIX), BF16),
            pltpu.VMEM((OWN_P,), jnp.int32),
            pltpu.VMEM((RADII, HARM), F32),
            pltpu.VMEM((OWN_R, HARM), BF16),
            pltpu.VMEM(syn.shape, BF16),
            pltpu.VMEM(fwd.shape, BF16),
            pltpu.VMEM((PIX, OWN_P), BF16),
            pltpu.VMEM((NBLK, BLK, OWN_R), F32),
            pltpu.VMEM((PIX, OWN_R), BF16),
            pltpu.VMEM((PT, OWN_R, 128), F32),
            pltpu.VMEM((NQ, OWN_R, 128), BF16),
            pltpu.VMEM((OWN_P, OWN_R), BF16),
            pltpu.VMEM((ORD // 2, 2, RADII, OWN_R), F32),
            pltpu.VMEM((8, 128), F32),
            pltpu.VMEM((NQ - 1, 8, 128), F32),
            pltpu.VMEM((8, 128), F32),
            pltpu.VMEM((8, 128), F32),
            pltpu.VMEM((1, 128), F32),
            pltpu.VMEM((NX - 1, 1, 128), F32),
            pltpu.VMEM((1, 128), F32),
            pltpu.VMEM((NZ - 1, 1, 128), F32),
            pltpu.VMEM((NQ, NX, 16, 128), BF16),
            pltpu.VMEM((PLANE - 1, 16, 128), BF16),
            pltpu.VMEM((16, 128), F32),
            pltpu.VMEM((RING, 1, 128), F32),
            pltpu.VMEM((RING - 1, 1, 128), F32),
        ]
        + [dma(())] * 18,
        compiler_params=pltpu.CompilerParams(collective_id=0, has_side_effects=True),
        name="recover",
    )(patterns, mask, model.T, wigner, jnp.asarray(syn), jnp.asarray(fwd))
    return out.T


def solution(mesh):
    return jax.shard_map(
        local,
        mesh=mesh,
        in_specs=(P("pat", None), P("pat"), P(), P("ori", None)),
        out_specs=P("ori", "pat"),
        check_vma=False,
    )
```

```python
import math

import jax
import jax.numpy as jnp
import numpy as np
from jax import lax
from jax.experimental import pallas as pl
from jax.experimental.pallas import tpu as pltpu
from jax.sharding import PartitionSpec as P

RADII = 64
ANGLES = 64
DEG = 16
ORD = 64
PIX = 4096
HARM = 1024
PATTERNS = 12288
ORIENTS = 2048

TEMPER = 0.05
BACKGROUND = 0.1

NX, NZ = 4, 8
NH, NQ = 2, 8
PLANE = NX * NQ
RING = NH * NZ
OWN_P = PATTERNS // (NX * NZ)
OWN_R = ORIENTS // (NH * NQ)
PT = OWN_P // 128
BLK = 4 * ANGLES
NBLK = PIX // BLK

F32 = jnp.float32
BF16 = jnp.bfloat16
MESH = pl.DeviceIdType.MESH


def order_table():
    orders = np.arange(ORD)[:, None]
    angles = np.arange(ANGLES)[None, :]
    half = ANGLES // 2
    step = 2.0 * math.pi / ANGLES
    cos = np.cos(step * ((orders * angles) % ANGLES))
    sin = np.sin(step * (((orders - half) * angles) % ANGLES))
    return np.where(orders <= half, cos, sin).astype(np.float32)


def terms(full):
    high = full.astype(BF16)
    low = (full - high.astype(np.float32)).astype(BF16)
    return np.concatenate([high, high, low], axis=1)


def tables():
    table = order_table()
    eye = np.eye(4, dtype=np.float32)
    syn = np.einsum("ka,bc->bakc", table, eye).reshape(BLK, BLK)
    fwd = np.einsum("ka,bc->kbca", table * np.float32(2.0 / ANGLES), eye)
    swap = fwd[np.arange(ORD) ^ 1]
    return (
        terms(syn),
        np.stack([terms(fwd.reshape(BLK, BLK)), terms(swap.reshape(BLK, BLK))]),
    )


def split(value):
    high = value.astype(BF16)
    low = (value - high.astype(F32)).astype(BF16)
    return high, low


def dot(a, b):
    return jnp.dot(a, b, preferred_element_type=F32)


def apply_table(table, one, two):
    high, low = split(jnp.concatenate([one, two], axis=1))
    out = dot(table, jnp.concatenate([high, low, high], axis=0))
    return out[:, :OWN_R], out[:, OWN_R:]


def far_first(n):
    return sorted(range(1, n), key=lambda j: -min(j, n - j))


def kernel(
    pat_hbm, mask_hbm, model_hbm, wig_hbm, syn_hbm, fwd_hbm, out_ref,
    pat, mask, model, wig, syn, fwd,
    pat_t, cyc, logs, score, wig_p, wt, ordt,
    stat, b1, pair, b2, occ1, c1, harm, e1, zsum, zsend, e2,
    pat_sem, mask_sem, model_sem, wig_sem, syn_sem, fwd_sem,
    b1_s, b1_r, b2_s, b2_r, c1_s, c1_r, e1_s, e1_r, e2_s, e2_r,
):
    p_id = lax.axis_index("pat")
    o_id = lax.axis_index("ori")
    x, zl = lax.div(p_id, NZ), lax.rem(p_id, NZ)
    zh, q = lax.div(o_id, NQ), lax.rem(o_id, NQ)
    z = zh * NZ + zl

    def plane_peer(dx, dq):
        return (lax.rem(x + dx, NX) * NZ + zl, zh * NQ + lax.rem(q + dq, NQ))

    def ring_peer(dz):
        far = lax.rem(z + dz, RING)
        return (x * NZ + lax.rem(far, NZ), lax.div(far, NZ) * NQ + q)

    def pat_peer(dx, dz):
        return (lax.rem(x + dx, NX) * NZ + lax.rem(zl + dz, NZ), o_id)

    pat_peers = [(dx, dz) for dz in far_first(NZ) + [0] for dx in (2, 1, 3, 0) if dx or dz]

    def greet(peer):
        pl.semaphore_signal(barrier, inc=1, device_id=peer, device_id_type=MESH)

    def send(src, dst, ssem, rsem, peer):
        pltpu.make_async_remote_copy(
            src_ref=src, dst_ref=dst, send_sem=ssem, recv_sem=rsem,
            device_id=peer, device_id_type=MESH,
        ).start()

    def whole(buf, ssem, rsem, peer):
        return pltpu.make_async_remote_copy(
            src_ref=buf, dst_ref=buf, send_sem=ssem, recv_sem=rsem,
            device_id=peer, device_id_type=MESH,
        )

    loads = [
        pltpu.make_async_copy(*refs)
        for refs in (
            (model_hbm, model, model_sem), (wig_hbm, wig, wig_sem), (syn_hbm, syn, syn_sem),
            (pat_hbm, pat, pat_sem), (fwd_hbm, fwd, fwd_sem), (mask_hbm, mask, mask_sem),
        )
    ]
    model_in, wig_in, syn_in, pat_in, fwd_in, mask_in = loads
    for load in loads:
        load.start()

    barrier = pltpu.get_barrier_semaphore()
    greet(ring_peer(NZ))
    for dx, dz in pat_peers:
        greet(pat_peer(dx, dz))
    for j in far_first(NQ):
        greet(plane_peer(0, j))

    row = lax.broadcasted_iota(jnp.int32, (16, 128), 0)
    lane = lax.broadcasted_iota(jnp.int32, (16, 128), 1)
    own = [
        jnp.where(lax.div(lane, DEG) == lax.div(row, 4) + n, 1.0, 0.0).astype(BF16)
        for n in (0, 4)
    ]
    upper = lax.broadcasted_iota(jnp.int32, (1, 8, 128), 1) < 4
    model_in.wait()
    wig_in.wait()

    def spread(value):
        tile = value.reshape(RADII // 8, 8, 128)
        other = pltpu.roll(tile, 4, 1)
        one = jnp.where(upper, tile, other)
        two = jnp.where(upper, other, tile)
        rows = []
        for i in range(RADII // 8):
            for half in (one[i], two[i]):
                packed = jnp.concatenate([half, half], axis=0).astype(BF16)
                rows += [packed * own[0], packed * own[1]]
        return jnp.concatenate(rows, axis=0)

    def gather_cycles(g):
        cols = pl.ds(pl.multiple_of(g * 128, 128), 128)
        m = model[:, cols]
        high = m.astype(BF16).astype(F32)
        left = jnp.concatenate([spread(high), spread(m - high)], axis=1)
        w = wig[:, cols]
        out = lax.dot_general(
            left, jnp.concatenate([w, w], axis=1), (((1,), (1,)), ((), ())),
            preferred_element_type=F32,
        )
        cyc[:, pl.ds(pl.multiple_of(g * 32, 32), 32), :] = out.reshape(NBLK, 32, OWN_R)

    @pl.loop(0, 2)
    def _(h):
        for n in range(ORD // 16):
            gather_cycles(h * (ORD // 16) + n)

    syn_in.wait()

    def expand(h, total):
        for m in range(0, NBLK // 2, 2):
            j = h * (NBLK // 2) + m
            for n, part in enumerate(apply_table(syn[...], cyc[j], cyc[j + 1])):
                value = (BACKGROUND + part).astype(BF16)
                logs[pl.ds(pl.multiple_of((j + n) * BLK, BLK), BLK), :] = value
                e = jnp.exp(value.astype(F32))
                total = total + jnp.sum(e.reshape(BLK // 8, 8, OWN_R), axis=0)
        return total

    total = lax.fori_loop(0, 2, expand, jnp.zeros((8, OWN_R), F32))
    intensity = jnp.sum(total, axis=0, keepdims=True)

    pat_in.wait()
    scaled = TEMPER * (dot(pat[...], logs[...]) - intensity)
    for t in range(PT):
        score[t] = scaled[t * 128:(t + 1) * 128, :].T
    peaks, masses = [], []
    for t in range(PT):
        s = score[t]
        m = jnp.max(s, axis=0, keepdims=True)
        peaks.append(m)
        masses.append(jnp.sum(jnp.exp(s - m), axis=0, keepdims=True))
    blank = jnp.zeros((8 - 2 * PT, 128), F32)
    stat[...] = jnp.concatenate(peaks + masses + [blank], axis=0)

    pl.semaphore_wait(barrier, 1 + NX * NZ - 1 + NQ - 1)

    for j in far_first(NQ):
        send(stat, b1.at[j - 1], b1_s, b1_r, plane_peer(0, j))

    fwd_in.wait()
    mask_in.wait()
    low_half = lax.broadcasted_iota(jnp.int32, (OWN_R, 128), 1) < 64
    for t in range(NQ // 2):
        a = wig[:, t * 128:(t + 1) * 128].astype(F32)
        b = wig[:, 512 + t * 128:512 + (t + 1) * 128].astype(F32)
        wig_p[2 * t] = jnp.where(low_half, a, pltpu.roll(b, 64, 1)).astype(BF16)
        wig_p[2 * t + 1] = jnp.where(low_half, pltpu.roll(a, 64, 1), b).astype(BF16)

    b1_all = whole(b1, b1_s, b1_r, plane_peer(0, 1))
    b1_all.wait_recv()
    peak = stat[0:PT, :]
    for j in range(NQ - 1):
        peak = jnp.maximum(peak, b1[j, 0:PT, :])
    mass = stat[PT:2 * PT, :] * jnp.exp(stat[0:PT, :] - peak)
    for j in range(NQ - 1):
        mass = mass + b1[j, PT:2 * PT, :] * jnp.exp(b1[j, 0:PT, :] - peak)
    pair[...] = jnp.concatenate([peak, mass, blank], axis=0)
    send(pair, b2, b2_s, b2_r, ring_peer(NZ))

    @pl.loop(0, PIX // 128)
    def _(j):
        span = pl.ds(pl.multiple_of(j * 128, 128), 128)
        pat_t[span, :] = pat[:, span].T

    b2_all = whole(b2, b2_s, b2_r, ring_peer(NZ))
    b2_all.wait_recv()
    far_peak = b2[0:PT, :]
    top = jnp.maximum(peak, far_peak)
    mass = mass * jnp.exp(peak - top) + b2[PT:2 * PT, :] * jnp.exp(far_peak - top)
    part = jnp.zeros((8, OWN_R), F32)
    for t in range(PT):
        counts = mask[t * 128:(t + 1) * 128].astype(F32).reshape(1, 128)
        factor = counts / mass[t:t + 1, :]
        w = (jnp.exp(score[t] - top[t:t + 1, :]) * factor).T.astype(BF16)
        wt[t * 128:(t + 1) * 128, :] = w
        part = part + jnp.sum(w.astype(F32).reshape(16, 8, OWN_R), axis=0)
    occ1[...] = jnp.sum(part, axis=0, keepdims=True)

    for dx, dz in pat_peers:
        send(occ1, c1.at[dx * NZ + dz - 1], c1_s, c1_r, pat_peer(dx, dz))

    def compress(i, carry):
        rows = [pl.ds(pl.multiple_of((4 * i + n) * BLK, BLK), BLK) for n in range(4)]
        sums = [dot(pat_t[r, :], wt[...]) for r in rows]
        evens = apply_table(fwd[0], sums[0], sums[2])
        odds = apply_table(fwd[1], sums[1], sums[3])
        one, two = (
            [v.reshape(ORD // 2, 8, OWN_R) for v in side] for side in (evens, odds)
        )
        cols = pl.ds(pl.multiple_of(i * 16, 16), 16)
        for par in range(2):
            whole_tile = jnp.concatenate(
                [jnp.where(upper, *((a, b) if par == 0 else (b, a))) for a, b in zip(one, two)],
                axis=1,
            )
            high, low = split(whole_tile)
            ordt[:, par, cols, 0:128] = high
            ordt[:, par, cols, 128:256] = low
        return carry

    lax.fori_loop(0, NBLK // 4, compress, 0)
    c1_all = whole(c1, c1_s, c1_r, pat_peer(1, 0))
    c1_all.wait_recv()
    occ = occ1[...] + jnp.sum(c1[...], axis=0)
    inv = (1.0 / math.sqrt(ORIENTS)) / (occ + 1.0)

    slot = lax.div(lax.broadcasted_iota(jnp.int32, (RADII, 128), 1), DEG)

    inv_rows = jnp.broadcast_to(inv, (OWN_R, OWN_R)).T
    for n in range(NQ):
        wig_p[n] = (wig_p[n].astype(F32) * inv_rows).astype(BF16)

    def project(i):
        g = lax.rem(q + i, NQ)
        w = wig_p[g]
        both = jnp.concatenate([w, w], axis=0)
        left = [
            ordt[pl.ds(h * (ORD // 4) + g * 2, 2)].reshape(BLK, 2 * OWN_R) for h in range(2)
        ]
        return dot(jnp.concatenate(left, axis=0), both)

    def share(i, out):
        g = lax.rem(q + i, NQ)
        acc = [jnp.zeros((RADII, 128), F32)] * 2
        for kk in range(8):
            acc[kk % 2] = jnp.where(slot == kk, out[kk * RADII:(kk + 1) * RADII, :], acc[kk % 2])
        odd = pltpu.roll(acc[1].reshape(RADII // 8, 8, 128), 4, 1).reshape(RADII, 128)
        harm[g] = (acc[0] + odd).astype(BF16).reshape(NX, 16, 128)
        for dx in (2, 1, 3, 0):
            if dx or i:
                send(
                    harm.at[g, lax.rem(x + dx, NX)], e1.at[dx * NQ + i - 1], e1_s, e1_r,
                    plane_peer(dx, i),
                )

    order = far_first(NQ) + [0]
    out = project(order[0])
    for i, later in zip(order, order[1:] + [None]):
        coming = None if later is None else project(later)
        share(i, out)
        out = coming
    e1_all = whole(e1, e1_s, e1_r, plane_peer(1, 0))
    e1_all.wait_recv()
    tot = harm[q, x].astype(F32)
    for j in range(PLANE - 1):
        tot = tot + e1[j].astype(F32)
    zsum[...] = tot
    even = zsum[pl.ds(0, 8, stride=2), :]
    odd = zsum[pl.ds(1, 8, stride=2), :]
    first = lane[:8] < 64
    rows = jnp.concatenate(
        [
            jnp.where(first, even, pltpu.roll(odd, 64, 1)),
            jnp.where(first, pltpu.roll(even, 64, 1), odd),
        ],
        axis=0,
    )
    for j in range(RING):
        zsend[j] = rows[j:j + 1, :]
    for j in far_first(RING):
        send(zsend.at[lax.rem(z + j, RING)], e2.at[j - 1], e2_s, e2_r, ring_peer(j))
    e2_all = whole(e2, e2_s, e2_r, ring_peer(1))
    e2_all.wait_recv()
    fin = zsend[z]
    for j in range(RING - 1):
        fin = fin + e2[j]
    out_ref[0:1, :] = fin[:, :64]
    out_ref[1:2, :] = fin[:, 64:]
    for copies in (b1_all, c1_all, e1_all, e2_all):
        copies.wait_send()
    pltpu.make_async_remote_copy(
        src_ref=pair, dst_ref=b2, send_sem=b2_s, recv_sem=b2_r,
        device_id=ring_peer(NZ), device_id_type=MESH,
    ).wait_send()


def local(patterns, mask, model, wigner):
    syn, fwd = tables()
    hbm = pl.BlockSpec(memory_space=pl.ANY)
    dma = pltpu.SemaphoreType.DMA
    out = pl.pallas_call(
        kernel,
        out_shape=jax.ShapeDtypeStruct((2, 64), F32),
        in_specs=[hbm] * 6,
        out_specs=pl.BlockSpec(memory_space=pltpu.VMEM),
        scratch_shapes=[
            pltpu.VMEM((OWN_P, PIX), BF16),
            pltpu.VMEM((OWN_P,), jnp.int32),
            pltpu.VMEM((RADII, HARM), F32),
            pltpu.VMEM((OWN_R, HARM), BF16),
            pltpu.VMEM(syn.shape, BF16),
            pltpu.VMEM(fwd.shape, BF16),
            pltpu.VMEM((PIX, OWN_P), BF16),
            pltpu.VMEM((NBLK, BLK, OWN_R), F32),
            pltpu.VMEM((PIX, OWN_R), BF16),
            pltpu.VMEM((PT, OWN_R, 128), F32),
            pltpu.VMEM((NQ, OWN_R, 128), BF16),
            pltpu.VMEM((OWN_P, OWN_R), BF16),
            pltpu.VMEM((ORD // 2, 2, RADII, 2 * OWN_R), BF16),
            pltpu.VMEM((8, 128), F32),
            pltpu.VMEM((NQ - 1, 8, 128), F32),
            pltpu.VMEM((8, 128), F32),
            pltpu.VMEM((8, 128), F32),
            pltpu.VMEM((1, 128), F32),
            pltpu.VMEM((NX * NZ - 1, 1, 128), F32),
            pltpu.VMEM((NQ, NX, 16, 128), BF16),
            pltpu.VMEM((PLANE - 1, 16, 128), BF16),
            pltpu.VMEM((16, 128), F32),
            pltpu.VMEM((RING, 1, 128), F32),
            pltpu.VMEM((RING - 1, 1, 128), F32),
        ]
        + [dma(())] * 16,
        compiler_params=pltpu.CompilerParams(collective_id=0, has_side_effects=True),
        name="recover",
    )(patterns, mask, model.T, wigner, jnp.asarray(syn), jnp.asarray(fwd))
    return out.T


def solution(mesh):
    return jax.shard_map(
        local,
        mesh=mesh,
        in_specs=(P("pat", None), P("pat"), P(), P("ori", None)),
        out_specs=P("ori", "pat"),
        check_vma=False,
    )
```

```python
import math

import jax
import jax.numpy as jnp
import numpy as np
from jax import lax
from jax.experimental import pallas as pl
from jax.experimental.pallas import tpu as pltpu
from jax.sharding import PartitionSpec as P

RADII = 64
ANGLES = 64
DEG = 16
ORD = 64
PIX = 4096
HARM = 1024
PATTERNS = 12288
ORIENTS = 2048

TEMPER = 0.05
BACKGROUND = 0.1

NX, NZ = 4, 8
NH, NQ = 2, 8
PLANE = NX * NQ
RING = NH * NZ
OWN_P = PATTERNS // (NX * NZ)
OWN_R = ORIENTS // (NH * NQ)
PT = OWN_P // 128
BLK = 4 * ANGLES
NBLK = PIX // BLK

F32 = jnp.float32
BF16 = jnp.bfloat16
MESH = pl.DeviceIdType.MESH


def order_table():
    orders = np.arange(ORD)[:, None]
    angles = np.arange(ANGLES)[None, :]
    half = ANGLES // 2
    step = 2.0 * math.pi / ANGLES
    cos = np.cos(step * ((orders * angles) % ANGLES))
    sin = np.sin(step * (((orders - half) * angles) % ANGLES))
    return np.where(orders <= half, cos, sin).astype(np.float32)


def terms(full):
    high = full.astype(BF16)
    low = (full - high.astype(np.float32)).astype(BF16)
    return np.concatenate([high, high, low], axis=1)


def tables():
    table = order_table()
    eye = np.eye(4, dtype=np.float32)
    syn = np.einsum("ka,bc->bakc", table, eye).reshape(BLK, BLK)
    fwd = np.einsum("ka,bc->kbca", table * np.float32(2.0 / ANGLES), eye)
    swap = fwd[np.arange(ORD) ^ 1]
    return (
        terms(syn),
        np.stack([terms(fwd.reshape(BLK, BLK)), terms(swap.reshape(BLK, BLK))]),
    )


def split(value):
    high = value.astype(BF16)
    low = (value - high.astype(F32)).astype(BF16)
    return high, low


def dot(a, b):
    return jnp.dot(a, b, preferred_element_type=F32)


def apply_table(table, one, two):
    high, low = split(jnp.concatenate([one, two], axis=1))
    out = dot(table, jnp.concatenate([high, low, high], axis=0))
    return out[:, :OWN_R], out[:, OWN_R:]


def far_first(n):
    return sorted(range(1, n), key=lambda j: -min(j, n - j))


def kernel(
    pat_hbm, mask_hbm, model_hbm, wig_hbm, syn_hbm, fwd_hbm, out_ref,
    pat, mask, model, wig, syn, fwd,
    pat_t, cyc, logs, score, wig_p, wt, ordt,
    stat, b1, pair, b2, occ1, c1, harm, e1, zsum, zsend, e2,
    pat_sem, mask_sem, model_sem, wig_sem, syn_sem, fwd_sem,
    b1_s, b1_r, b2_s, b2_r, c1_s, c1_r, e1_s, e1_r, e2_s, e2_r, known,
):
    p_id = lax.axis_index("pat")
    o_id = lax.axis_index("ori")
    x, zl = lax.div(p_id, NZ), lax.rem(p_id, NZ)
    zh, q = lax.div(o_id, NQ), lax.rem(o_id, NQ)
    z = zh * NZ + zl

    def plane_peer(dx, dq):
        return (lax.rem(x + dx, NX) * NZ + zl, zh * NQ + lax.rem(q + dq, NQ))

    def ring_peer(dz):
        far = lax.rem(z + dz, RING)
        return (x * NZ + lax.rem(far, NZ), lax.div(far, NZ) * NQ + q)

    def pat_peer(dx, dz):
        return (lax.rem(x + dx, NX) * NZ + lax.rem(zl + dz, NZ), o_id)

    pat_peers = [(dx, dz) for dz in far_first(NZ) + [0] for dx in (2, 1, 3, 0) if dx or dz]

    def greet(peer):
        pl.semaphore_signal(barrier, inc=1, device_id=peer, device_id_type=MESH)

    def send(src, dst, ssem, rsem, peer):
        pltpu.make_async_remote_copy(
            src_ref=src, dst_ref=dst, send_sem=ssem, recv_sem=rsem,
            device_id=peer, device_id_type=MESH,
        ).start()

    def whole(buf, ssem, rsem, peer):
        return pltpu.make_async_remote_copy(
            src_ref=buf, dst_ref=buf, send_sem=ssem, recv_sem=rsem,
            device_id=peer, device_id_type=MESH,
        )

    loads = [
        pltpu.make_async_copy(*refs)
        for refs in (
            (model_hbm, model, model_sem), (wig_hbm, wig, wig_sem), (syn_hbm, syn, syn_sem),
            (pat_hbm, pat, pat_sem), (fwd_hbm, fwd, fwd_sem), (mask_hbm, mask, mask_sem),
        )
    ]
    model_in, wig_in, syn_in, pat_in, fwd_in, mask_in = loads
    for load in loads:
        load.start()

    barrier = pltpu.get_barrier_semaphore()
    greet(ring_peer(NZ))
    for dx, dz in pat_peers:
        if dx == 0 or dz == 0:
            greet(pat_peer(dx, dz))
    for j in far_first(NQ):
        greet(plane_peer(0, j))

    row = lax.broadcasted_iota(jnp.int32, (16, 128), 0)
    lane = lax.broadcasted_iota(jnp.int32, (16, 128), 1)
    own = [
        jnp.where(lax.div(lane, DEG) == lax.div(row, 4) + n, 1.0, 0.0).astype(BF16)
        for n in (0, 4)
    ]
    upper = lax.broadcasted_iota(jnp.int32, (1, 8, 128), 1) < 4
    model_in.wait()
    wig_in.wait()

    def spread(value):
        tile = value.reshape(RADII // 8, 8, 128)
        other = pltpu.roll(tile, 4, 1)
        one = jnp.where(upper, tile, other)
        two = jnp.where(upper, other, tile)
        rows = []
        for i in range(RADII // 8):
            for half in (one[i], two[i]):
                packed = jnp.concatenate([half, half], axis=0).astype(BF16)
                rows += [packed * own[0], packed * own[1]]
        return jnp.concatenate(rows, axis=0)

    def gather_cycles(g):
        cols = pl.ds(pl.multiple_of(g * 128, 128), 128)
        m = model[:, cols]
        high = m.astype(BF16).astype(F32)
        left = jnp.concatenate([spread(high), spread(m - high)], axis=1)
        w = wig[:, cols]
        out = lax.dot_general(
            left, jnp.concatenate([w, w], axis=1), (((1,), (1,)), ((), ())),
            preferred_element_type=F32,
        )
        cyc[:, pl.ds(pl.multiple_of(g * 32, 32), 32), :] = out.reshape(NBLK, 32, OWN_R)

    @pl.loop(0, 2)
    def _(h):
        for n in range(ORD // 16):
            gather_cycles(h * (ORD // 16) + n)

    syn_in.wait()

    def expand(h, total):
        for m in range(0, NBLK // 2, 2):
            j = h * (NBLK // 2) + m
            for n, part in enumerate(apply_table(syn[...], cyc[j], cyc[j + 1])):
                value = (BACKGROUND + part).astype(BF16)
                logs[pl.ds(pl.multiple_of((j + n) * BLK, BLK), BLK), :] = value
                e = jnp.exp(value.astype(F32))
                total = total + jnp.sum(e.reshape(BLK // 8, 8, OWN_R), axis=0)
        return total

    total = lax.fori_loop(0, 2, expand, jnp.zeros((8, OWN_R), F32))
    intensity = jnp.sum(total, axis=0, keepdims=True)

    pat_in.wait()
    scaled = TEMPER * (dot(pat[...], logs[...]) - intensity)
    for t in range(PT):
        score[t] = scaled[t * 128:(t + 1) * 128, :].T
    peaks, masses = [], []
    for t in range(PT):
        s = score[t]
        m = jnp.max(s, axis=0, keepdims=True)
        peaks.append(m)
        masses.append(jnp.sum(jnp.exp(s - m), axis=0, keepdims=True))
    blank = jnp.zeros((8 - 2 * PT, 128), F32)
    stat[...] = jnp.concatenate(peaks + masses + [blank], axis=0)

    pl.semaphore_wait(barrier, 1 + NX - 1 + NZ - 1 + NQ - 1)

    for j in far_first(NQ):
        send(stat, b1.at[j - 1], b1_s, b1_r, plane_peer(0, j))

    for dx in far_first(NX):
        pl.semaphore_signal(known, inc=1, device_id=pat_peer(dx, 0), device_id_type=MESH)

    fwd_in.wait()
    mask_in.wait()
    low_half = lax.broadcasted_iota(jnp.int32, (OWN_R, 128), 1) < 64
    for t in range(NQ // 2):
        a = wig[:, t * 128:(t + 1) * 128].astype(F32)
        b = wig[:, 512 + t * 128:512 + (t + 1) * 128].astype(F32)
        wig_p[2 * t] = jnp.where(low_half, a, pltpu.roll(b, 64, 1)).astype(BF16)
        wig_p[2 * t + 1] = jnp.where(low_half, pltpu.roll(a, 64, 1), b).astype(BF16)

    b1_all = whole(b1, b1_s, b1_r, plane_peer(0, 1))
    b1_all.wait_recv()
    peak = stat[0:PT, :]
    for j in range(NQ - 1):
        peak = jnp.maximum(peak, b1[j, 0:PT, :])
    mass = stat[PT:2 * PT, :] * jnp.exp(stat[0:PT, :] - peak)
    for j in range(NQ - 1):
        mass = mass + b1[j, PT:2 * PT, :] * jnp.exp(b1[j, 0:PT, :] - peak)
    pair[...] = jnp.concatenate([peak, mass, blank], axis=0)
    send(pair, b2, b2_s, b2_r, ring_peer(NZ))

    @pl.loop(0, PIX // 128)
    def _(j):
        span = pl.ds(pl.multiple_of(j * 128, 128), 128)
        pat_t[span, :] = pat[:, span].T

    b2_all = whole(b2, b2_s, b2_r, ring_peer(NZ))
    b2_all.wait_recv()
    far_peak = b2[0:PT, :]
    top = jnp.maximum(peak, far_peak)
    mass = mass * jnp.exp(peak - top) + b2[PT:2 * PT, :] * jnp.exp(far_peak - top)
    part = jnp.zeros((8, OWN_R), F32)
    for t in range(PT):
        counts = mask[t * 128:(t + 1) * 128].astype(F32).reshape(1, 128)
        factor = counts / mass[t:t + 1, :]
        w = (jnp.exp(score[t] - top[t:t + 1, :]) * factor).T.astype(BF16)
        wt[t * 128:(t + 1) * 128, :] = w
        part = part + jnp.sum(w.astype(F32).reshape(16, 8, OWN_R), axis=0)
    occ1[...] = jnp.sum(part, axis=0, keepdims=True)

    pl.semaphore_wait(known, NX - 1)
    for dx, dz in pat_peers:
        send(occ1, c1.at[dx * NZ + dz - 1], c1_s, c1_r, pat_peer(dx, dz))

    def compress(i, carry):
        rows = [pl.ds(pl.multiple_of((4 * i + n) * BLK, BLK), BLK) for n in range(4)]
        sums = [dot(pat_t[r, :], wt[...]) for r in rows]
        evens = apply_table(fwd[0], sums[0], sums[2])
        odds = apply_table(fwd[1], sums[1], sums[3])
        one, two = (
            [v.reshape(ORD // 2, 8, OWN_R) for v in side] for side in (evens, odds)
        )
        cols = pl.ds(pl.multiple_of(i * 16, 16), 16)
        for par in range(2):
            whole_tile = jnp.concatenate(
                [jnp.where(upper, *((a, b) if par == 0 else (b, a))) for a, b in zip(one, two)],
                axis=1,
            )
            for h in range(NH):
                half = whole_tile[h * (ORD // 4):(h + 1) * (ORD // 4)]
                ordt[:, par, cols, h * OWN_R:(h + 1) * OWN_R] = half.astype(BF16)
        return carry

    lax.fori_loop(0, NBLK // 4, compress, 0)
    c1_all = whole(c1, c1_s, c1_r, pat_peer(1, 0))
    c1_all.wait_recv()
    occ = occ1[...] + jnp.sum(c1[...], axis=0)
    inv = (1.0 / math.sqrt(ORIENTS)) / (occ + 1.0)

    slot = lax.rem(lax.div(lax.broadcasted_iota(jnp.int32, (RADII, 128), 1), DEG), 4)

    inv_rows = jnp.broadcast_to(inv, (OWN_R, OWN_R)).T

    def project(i):
        g = lax.rem(q + i, NQ)
        w = wig_p[g].astype(F32) * inv_rows
        both = jnp.concatenate([jnp.where(low_half, w, 0.0), jnp.where(low_half, 0.0, w)], axis=0)
        return dot(ordt[pl.ds(g * 2, 2)].reshape(BLK, 2 * OWN_R), both.astype(BF16))

    def share(i, out):
        g = lax.rem(q + i, NQ)
        acc = [jnp.zeros((RADII, 128), F32)] * 2
        for kk in range(4):
            acc[kk % 2] = jnp.where(slot == kk, out[kk * RADII:(kk + 1) * RADII, :], acc[kk % 2])
        odd = pltpu.roll(acc[1].reshape(RADII // 8, 8, 128), 4, 1).reshape(RADII, 128)
        harm[g] = (acc[0] + odd).astype(BF16).reshape(NX, 16, 128)
        for dx in (2, 1, 3, 0):
            if dx or i:
                send(
                    harm.at[g, lax.rem(x + dx, NX)], e1.at[dx * NQ + i - 1], e1_s, e1_r,
                    plane_peer(dx, i),
                )

    order = far_first(NQ) + [0]
    out = project(order[0])
    for i, later in zip(order, order[1:] + [None]):
        coming = None if later is None else project(later)
        share(i, out)
        out = coming
    e1_all = whole(e1, e1_s, e1_r, plane_peer(1, 0))
    e1_all.wait_recv()
    tot = harm[q, x].astype(F32)
    for j in range(PLANE - 1):
        tot = tot + e1[j].astype(F32)
    zsum[...] = tot
    even = zsum[pl.ds(0, 8, stride=2), :]
    odd = zsum[pl.ds(1, 8, stride=2), :]
    first = lane[:8] < 64
    rows = jnp.concatenate(
        [
            jnp.where(first, even, pltpu.roll(odd, 64, 1)),
            jnp.where(first, pltpu.roll(even, 64, 1), odd),
        ],
        axis=0,
    )
    for j in range(RING):
        zsend[j] = rows[j:j + 1, :]
    for j in far_first(RING):
        send(zsend.at[lax.rem(z + j, RING)], e2.at[j - 1], e2_s, e2_r, ring_peer(j))
    e2_all = whole(e2, e2_s, e2_r, ring_peer(1))
    e2_all.wait_recv()
    fin = zsend[z]
    for j in range(RING - 1):
        fin = fin + e2[j]
    out_ref[0:1, :] = fin[:, :64]
    out_ref[1:2, :] = fin[:, 64:]
    for copies in (b1_all, c1_all, e1_all, e2_all):
        copies.wait_send()
    pltpu.make_async_remote_copy(
        src_ref=pair, dst_ref=b2, send_sem=b2_s, recv_sem=b2_r,
        device_id=ring_peer(NZ), device_id_type=MESH,
    ).wait_send()


def local(patterns, mask, model, wigner):
    syn, fwd = tables()
    hbm = pl.BlockSpec(memory_space=pl.ANY)
    dma = pltpu.SemaphoreType.DMA
    out = pl.pallas_call(
        kernel,
        out_shape=jax.ShapeDtypeStruct((2, 64), F32),
        in_specs=[hbm] * 6,
        out_specs=pl.BlockSpec(memory_space=pltpu.VMEM),
        scratch_shapes=[
            pltpu.VMEM((OWN_P, PIX), BF16),
            pltpu.VMEM((OWN_P,), jnp.int32),
            pltpu.VMEM((RADII, HARM), F32),
            pltpu.VMEM((OWN_R, HARM), BF16),
            pltpu.VMEM(syn.shape, BF16),
            pltpu.VMEM(fwd.shape, BF16),
            pltpu.VMEM((PIX, OWN_P), BF16),
            pltpu.VMEM((NBLK, BLK, OWN_R), F32),
            pltpu.VMEM((PIX, OWN_R), BF16),
            pltpu.VMEM((PT, OWN_R, 128), F32),
            pltpu.VMEM((NQ, OWN_R, 128), BF16),
            pltpu.VMEM((OWN_P, OWN_R), BF16),
            pltpu.VMEM((ORD // 4, 2, RADII, 2 * OWN_R), BF16),
            pltpu.VMEM((8, 128), F32),
            pltpu.VMEM((NQ - 1, 8, 128), F32),
            pltpu.VMEM((8, 128), F32),
            pltpu.VMEM((8, 128), F32),
            pltpu.VMEM((1, 128), F32),
            pltpu.VMEM((NX * NZ - 1, 1, 128), F32),
            pltpu.VMEM((NQ, NX, 16, 128), BF16),
            pltpu.VMEM((PLANE - 1, 16, 128), BF16),
            pltpu.VMEM((16, 128), F32),
            pltpu.VMEM((RING, 1, 128), F32),
            pltpu.VMEM((RING - 1, 1, 128), F32),
        ]
        + [dma(())] * 16
        + [pltpu.SemaphoreType.REGULAR],
        compiler_params=pltpu.CompilerParams(collective_id=0, has_side_effects=True),
        name="recover",
    )(patterns, mask, model.T, wigner, jnp.asarray(syn), jnp.asarray(fwd))
    return out.T


def solution(mesh):
    return jax.shard_map(
        local,
        mesh=mesh,
        in_specs=(P("pat", None), P("pat"), P(), P("ori", None)),
        out_specs=P("ori", "pat"),
        check_vma=False,
    )
```

```python
import math

import jax
import jax.numpy as jnp
import numpy as np
from jax import lax
from jax.experimental import pallas as pl
from jax.experimental.pallas import tpu as pltpu
from jax.sharding import PartitionSpec as P

RADII = 64
ANGLES = 64
DEG = 16
ORD = 64
PIX = 4096
HARM = 1024
PATTERNS = 12288
ORIENTS = 2048

TEMPER = 0.05
BACKGROUND = 0.1

NX, NZ = 4, 8
NH, NQ = 2, 8
PLANE = NX * NQ
RING = NH * NZ
OWN_P = PATTERNS // (NX * NZ)
OWN_R = ORIENTS // (NH * NQ)
PT = OWN_P // 128
BLK = 4 * ANGLES
NBLK = PIX // BLK

F32 = jnp.float32
BF16 = jnp.bfloat16
MESH = pl.DeviceIdType.MESH


def order_table():
    orders = np.arange(ORD)[:, None]
    angles = np.arange(ANGLES)[None, :]
    half = ANGLES // 2
    step = 2.0 * math.pi / ANGLES
    cos = np.cos(step * ((orders * angles) % ANGLES))
    sin = np.sin(step * (((orders - half) * angles) % ANGLES))
    return np.where(orders <= half, cos, sin).astype(np.float32)


def terms(full):
    high = full.astype(BF16)
    low = (full - high.astype(np.float32)).astype(BF16)
    return np.concatenate([high, high, low], axis=1)


def tables():
    table = order_table()
    eye = np.eye(4, dtype=np.float32)
    syn = np.einsum("ka,bc->bakc", table, eye).reshape(BLK, BLK)
    fwd = np.einsum("ka,bc->kbca", table * np.float32(2.0 / ANGLES), eye)
    swap = fwd[np.arange(ORD) ^ 1]
    return (
        terms(syn),
        np.stack([terms(fwd.reshape(BLK, BLK)), terms(swap.reshape(BLK, BLK))]),
    )


def split(value):
    high = value.astype(BF16)
    low = (value - high.astype(F32)).astype(BF16)
    return high, low


def dot(a, b):
    return jnp.dot(a, b, preferred_element_type=F32)


def apply_table(table, one, two):
    high, low = split(jnp.concatenate([one, two], axis=1))
    out = dot(table, jnp.concatenate([high, low, high], axis=0))
    return out[:, :OWN_R], out[:, OWN_R:]


def far_first(n):
    return sorted(range(1, n), key=lambda j: -min(j, n - j))


def kernel(
    pat_hbm, mask_hbm, model_hbm, wig_hbm, syn_hbm, fwd_hbm, out_ref,
    pat, mask, model, wig, syn, fwd,
    pat_t, cyc, logs, score, wig_p, wt, ordt,
    stat, b1, pair, b2, occ1, c1, harm, e1, zsend, e2,
    pat_sem, mask_sem, model_sem, wig_sem, syn_sem, fwd_sem,
    b1_s, b1_r, b2_s, b2_r, c1_s, c1_r, e1_s, e1_r, e2_s, e2_r, known,
):
    p_id = lax.axis_index("pat")
    o_id = lax.axis_index("ori")
    x, zl = lax.div(p_id, NZ), lax.rem(p_id, NZ)
    zh, q = lax.div(o_id, NQ), lax.rem(o_id, NQ)
    z = zh * NZ + zl

    def plane_peer(dx, dq):
        return (xs[dx] * NZ + zl, zh * NQ + qs[dq])

    def ring_peer(dz):
        return (x * NZ + zls[dz % NZ], lax.div(zs[dz], NZ) * NQ + q)

    def pat_peer(dx, dz):
        return (xs[dx] * NZ + zls[dz], o_id)

    pat_peers = [(dx, dz) for dz in far_first(NZ) + [0] for dx in (2, 1, 3, 0) if dx or dz]

    def greet(peer):
        pl.semaphore_signal(barrier, inc=1, device_id=peer, device_id_type=MESH)

    def send(src, dst, ssem, rsem, peer):
        pltpu.make_async_remote_copy(
            src_ref=src, dst_ref=dst, send_sem=ssem, recv_sem=rsem,
            device_id=peer, device_id_type=MESH,
        ).start()

    def whole(buf, ssem, rsem, peer):
        return pltpu.make_async_remote_copy(
            src_ref=buf, dst_ref=buf, send_sem=ssem, recv_sem=rsem,
            device_id=peer, device_id_type=MESH,
        )

    loads = [
        pltpu.make_async_copy(*refs)
        for refs in (
            (model_hbm, model, model_sem), (wig_hbm, wig, wig_sem), (syn_hbm, syn, syn_sem),
            (pat_hbm, pat, pat_sem), (fwd_hbm, fwd, fwd_sem), (mask_hbm, mask, mask_sem),
        )
    ]
    model_in, wig_in, syn_in, pat_in, fwd_in, mask_in = loads
    for load in loads:
        load.start()

    barrier = pltpu.get_barrier_semaphore()
    greet((p_id, (1 - zh) * NQ + q))
    xs = [lax.rem(x + d, NX) for d in range(NX)]
    qs = [lax.rem(q + d, NQ) for d in range(NQ)]
    zls = [lax.rem(zl + d, NZ) for d in range(NZ)]
    for dx, dz in pat_peers:
        if dx == 0 or dz == 0:
            greet(pat_peer(dx, dz))
    for j in far_first(NQ):
        greet(plane_peer(0, j))

    row = lax.broadcasted_iota(jnp.int32, (16, 128), 0)
    lane = lax.broadcasted_iota(jnp.int32, (16, 128), 1)
    own = [
        jnp.where(lax.div(lane, DEG) == lax.div(row, 4) + n, 1.0, 0.0).astype(BF16)
        for n in (0, 4)
    ]
    upper = lax.broadcasted_iota(jnp.int32, (1, 8, 128), 1) < 4
    model_in.wait()
    wig_in.wait()

    def spread(value):
        tile = value.reshape(RADII // 8, 8, 128)
        other = pltpu.roll(tile, 4, 1)
        one = jnp.where(upper, tile, other)
        two = jnp.where(upper, other, tile)
        rows = []
        for i in range(RADII // 8):
            for half in (one[i], two[i]):
                packed = jnp.concatenate([half, half], axis=0).astype(BF16)
                rows += [packed * own[0], packed * own[1]]
        return jnp.concatenate(rows, axis=0)

    def gather_cycles(g):
        cols = pl.ds(pl.multiple_of(g * 128, 128), 128)
        m = model[:, cols]
        high = m.astype(BF16).astype(F32)
        left = jnp.concatenate([spread(high), spread(m - high)], axis=1)
        w = wig[:, cols]
        out = lax.dot_general(
            left, jnp.concatenate([w, w], axis=1), (((1,), (1,)), ((), ())),
            preferred_element_type=F32,
        )
        cyc[:, pl.ds(pl.multiple_of(g * 32, 32), 32), :] = out.reshape(NBLK, 32, OWN_R)

    @pl.loop(0, 2)
    def _(h):
        for n in range(ORD // 16):
            gather_cycles(h * (ORD // 16) + n)

    syn_in.wait()

    def expand(h, total):
        for m in range(0, NBLK // 2, 2):
            j = h * (NBLK // 2) + m
            for n, part in enumerate(apply_table(syn[...], cyc[j], cyc[j + 1])):
                value = (BACKGROUND + part).astype(BF16)
                logs[pl.ds(pl.multiple_of((j + n) * BLK, BLK), BLK), :] = value
                e = jnp.exp(value.astype(F32))
                total = total + jnp.sum(e.reshape(BLK // 8, 8, OWN_R), axis=0)
        return total

    total = lax.fori_loop(0, 2, expand, jnp.zeros((8, OWN_R), F32))
    intensity = jnp.sum(total, axis=0, keepdims=True)

    pat_in.wait()
    scaled = TEMPER * (dot(pat[...], logs[...]) - intensity)
    for t in range(PT):
        score[t] = scaled[t * 128:(t + 1) * 128, :].T
    peaks, masses = [], []
    for t in range(PT):
        s = score[t]
        m = jnp.max(s, axis=0, keepdims=True)
        peaks.append(m)
        masses.append(jnp.sum(jnp.exp(s - m), axis=0, keepdims=True))
    blank = jnp.zeros((8 - 2 * PT, 128), F32)
    stat[...] = jnp.concatenate(peaks + masses + [blank], axis=0)

    pl.semaphore_wait(barrier, 1 + NX - 1 + NZ - 1 + NQ - 1)

    for j in far_first(NQ):
        send(stat, b1.at[j - 1], b1_s, b1_r, plane_peer(0, j))

    for dx in far_first(NX):
        pl.semaphore_signal(known, inc=1, device_id=pat_peer(dx, 0), device_id_type=MESH)

    fwd_in.wait()
    mask_in.wait()
    low_half = lax.broadcasted_iota(jnp.int32, (OWN_R, 128), 1) < 64
    for t in range(NQ // 2):
        a = wig[:, t * 128:(t + 1) * 128].astype(F32)
        b = wig[:, 512 + t * 128:512 + (t + 1) * 128].astype(F32)
        wig_p[2 * t] = jnp.where(low_half, a, pltpu.roll(b, 64, 1)).astype(BF16)
        wig_p[2 * t + 1] = jnp.where(low_half, pltpu.roll(a, 64, 1), b).astype(BF16)

    b1_all = whole(b1, b1_s, b1_r, plane_peer(0, 1))
    b1_all.wait_recv()
    peak = stat[0:PT, :]
    for j in range(NQ - 1):
        peak = jnp.maximum(peak, b1[j, 0:PT, :])
    mass = stat[PT:2 * PT, :] * jnp.exp(stat[0:PT, :] - peak)
    for j in range(NQ - 1):
        mass = mass + b1[j, PT:2 * PT, :] * jnp.exp(b1[j, 0:PT, :] - peak)
    pair[...] = jnp.concatenate([peak, mass, blank], axis=0)
    send(pair, b2, b2_s, b2_r, (p_id, (1 - zh) * NQ + q))

    zs = [lax.rem(z + d, RING) for d in range(RING)]

    @pl.loop(0, PIX // 128)
    def _(j):
        span = pl.ds(pl.multiple_of(j * 128, 128), 128)
        pat_t[span, :] = pat[:, span].T

    b2_all = whole(b2, b2_s, b2_r, (p_id, (1 - zh) * NQ + q))
    b2_all.wait_recv()
    far_peak = b2[0:PT, :]
    top = jnp.maximum(peak, far_peak)
    mass = mass * jnp.exp(peak - top) + b2[PT:2 * PT, :] * jnp.exp(far_peak - top)
    part = jnp.zeros((8, OWN_R), F32)
    for t in range(PT):
        counts = mask[t * 128:(t + 1) * 128].astype(F32).reshape(1, 128)
        factor = counts / mass[t:t + 1, :]
        w = (jnp.exp(score[t] - top[t:t + 1, :]) * factor).T.astype(BF16)
        wt[t * 128:(t + 1) * 128, :] = w
        part = part + jnp.sum(w.astype(F32).reshape(16, 8, OWN_R), axis=0)
    occ1[...] = jnp.sum(part, axis=0, keepdims=True)

    pl.semaphore_wait(known, NX - 1)
    for dx, dz in pat_peers:
        send(occ1, c1.at[dx * NZ + dz - 1], c1_s, c1_r, pat_peer(dx, dz))

    def compress(i, carry):
        sums = []
        for n in range(4):
            first = n // 2 + 8 * (n % 2)
            rows = [
                pat_t[pl.ds(pl.multiple_of((16 * i + first + 2 * m) * ANGLES, ANGLES), ANGLES), :]
                for m in range(4)
            ]
            sums.append(dot(jnp.concatenate(rows, axis=0), wt[...]))
        evens = apply_table(fwd[0], sums[0], sums[2])
        odds = apply_table(fwd[1], sums[1], sums[3])
        one, two = (
            [v.reshape(ORD // 2, 8, OWN_R) for v in side] for side in (evens, odds)
        )
        cols = pl.ds(pl.multiple_of(i * 16, 16), 16)
        for par in range(2):
            whole_tile = jnp.concatenate(
                [jnp.where(upper, *((a, b) if par == 0 else (b, a))) for a, b in zip(one, two)],
                axis=1,
            )
            for h in range(NH):
                half = whole_tile[h * (ORD // 4):(h + 1) * (ORD // 4)]
                ordt[:, par, cols, h * OWN_R:(h + 1) * OWN_R] = half.astype(BF16)
        return carry

    lax.fori_loop(0, NBLK // 4, compress, 0)
    c1_all = whole(c1, c1_s, c1_r, pat_peer(1, 0))
    c1_all.wait_recv()
    occ = occ1[...] + jnp.sum(c1[...], axis=0)
    inv = (1.0 / math.sqrt(ORIENTS)) / (occ + 1.0)

    slot = lax.rem(lax.div(lax.broadcasted_iota(jnp.int32, (RADII, 128), 1), DEG), 4)

    inv_rows = jnp.broadcast_to(inv, (OWN_R, OWN_R)).T

    def project(i):
        g = qs[i]
        w = wig_p[g].astype(F32) * inv_rows
        both = jnp.concatenate([jnp.where(low_half, w, 0.0), jnp.where(low_half, 0.0, w)], axis=0)
        return dot(ordt[pl.ds(g * 2, 2)].reshape(BLK, 2 * OWN_R), both.astype(BF16))

    def share(i, out):
        g = qs[i]
        acc = [jnp.zeros((RADII, 128), F32)] * 2
        for kk in range(4):
            acc[kk % 2] = jnp.where(slot == kk, out[kk * RADII:(kk + 1) * RADII, :], acc[kk % 2])
        odd = pltpu.roll(acc[1].reshape(RADII // 8, 8, 128), 4, 1).reshape(RADII, 128)
        harm[g] = (acc[0] + odd).astype(BF16).reshape(NX, 16, 128)
        for dx in (2, 1, 3, 0):
            if dx or i:
                send(
                    harm.at[g, xs[dx]], e1.at[dx * NQ + i - 1], e1_s, e1_r,
                    plane_peer(dx, i),
                )

    order = far_first(NQ) + [0]
    ready = [project(order[0])]
    for n, i in enumerate(order):
        ready += [project(later) for later in order[len(ready):n + (3 if n else 2)]]
        share(i, ready[n])
    e1_all = whole(e1, e1_s, e1_r, plane_peer(1, 0))
    e1_all.wait_recv()
    tot = harm[q, x].astype(F32)
    for j in range(PLANE - 1):
        tot = tot + e1[j].astype(F32)
    even, odd = tot[:8], tot[8:]
    first = lane[:8] < 64
    rows = jnp.concatenate(
        [
            jnp.where(first, even, pltpu.roll(odd, 64, 1)),
            jnp.where(first, pltpu.roll(even, 64, 1), odd),
        ],
        axis=0,
    )
    for j in range(RING):
        zsend[j] = rows[j:j + 1, :]
    for j in far_first(RING):
        send(zsend.at[zs[j]], e2.at[j - 1], e2_s, e2_r, ring_peer(j))
    e2_all = whole(e2, e2_s, e2_r, ring_peer(1))
    e2_all.wait_recv()
    fin = zsend[z]
    for j in range(RING - 1):
        fin = fin + e2[j]
    out_ref[0:1, :] = fin[:, :64]
    out_ref[1:2, :] = fin[:, 64:]
    for copies in (b1_all, c1_all, e1_all, e2_all):
        copies.wait_send()
    pltpu.make_async_remote_copy(
        src_ref=pair, dst_ref=b2, send_sem=b2_s, recv_sem=b2_r,
        device_id=(p_id, (1 - zh) * NQ + q), device_id_type=MESH,
    ).wait_send()


def local(patterns, mask, model, wigner):
    syn, fwd = tables()
    hbm = pl.BlockSpec(memory_space=pltpu.MemorySpace.HBM)

    def in_hbm(value):
        return pltpu.with_memory_space_constraint(value, pltpu.MemorySpace.HBM)

    dma = pltpu.SemaphoreType.DMA
    out = pl.pallas_call(
        kernel,
        out_shape=jax.ShapeDtypeStruct((2, 64), F32),
        in_specs=[hbm] * 6,
        out_specs=pl.BlockSpec(memory_space=pltpu.VMEM),
        scratch_shapes=[
            pltpu.VMEM((OWN_P, PIX), BF16),
            pltpu.VMEM((OWN_P,), jnp.int32),
            pltpu.VMEM((RADII, HARM), F32),
            pltpu.VMEM((OWN_R, HARM), BF16),
            pltpu.VMEM(syn.shape, BF16),
            pltpu.VMEM(fwd.shape, BF16),
            pltpu.VMEM((PIX, OWN_P), BF16),
            pltpu.VMEM((NBLK, BLK, OWN_R), F32),
            pltpu.VMEM((PIX, OWN_R), BF16),
            pltpu.VMEM((PT, OWN_R, 128), F32),
            pltpu.VMEM((NQ, OWN_R, 128), BF16),
            pltpu.VMEM((OWN_P, OWN_R), BF16),
            pltpu.VMEM((ORD // 4, 2, RADII, 2 * OWN_R), BF16),
            pltpu.VMEM((8, 128), F32),
            pltpu.VMEM((NQ - 1, 8, 128), F32),
            pltpu.VMEM((8, 128), F32),
            pltpu.VMEM((8, 128), F32),
            pltpu.VMEM((1, 128), F32),
            pltpu.VMEM((NX * NZ - 1, 1, 128), F32),
            pltpu.VMEM((NQ, NX, 16, 128), BF16),
            pltpu.VMEM((PLANE - 1, 16, 128), BF16),
            pltpu.VMEM((RING, 1, 128), F32),
            pltpu.VMEM((RING - 1, 1, 128), F32),
        ]
        + [dma(())] * 16
        + [pltpu.SemaphoreType.REGULAR],
        compiler_params=pltpu.CompilerParams(
            collective_id=0, has_side_effects=True, vmem_limit_bytes=40 * 1024 * 1024
        ),
        name="recover",
    )(*(in_hbm(v) for v in (patterns, mask, model.T, wigner, jnp.asarray(syn), jnp.asarray(fwd))))
    return out.T


def solution(mesh):
    return jax.shard_map(
        local,
        mesh=mesh,
        in_specs=(P("pat", None), P("pat"), P(), P("ori", None)),
        out_specs=P("ori", "pat"),
        check_vma=False,
    )
```

```python
import math

import jax
import jax.numpy as jnp
import numpy as np
from jax import lax
from jax.experimental import pallas as pl
from jax.experimental.pallas import tpu as pltpu
from jax.sharding import PartitionSpec as P

RADII = 64
ANGLES = 64
DEG = 16
ORD = 64
PIX = 4096
HARM = 1024
PATTERNS = 12288
ORIENTS = 2048

TEMPER = 0.05
BACKGROUND = 0.1

NX, NZ = 4, 8
NH, NQ = 2, 8
PLANE = NX * NQ
RING = NH * NZ
OWN_P = PATTERNS // (NX * NZ)
OWN_R = ORIENTS // (NH * NQ)
PT = OWN_P // 128
BLK = 4 * ANGLES
NBLK = PIX // BLK

F32 = jnp.float32
BF16 = jnp.bfloat16
MESH = pl.DeviceIdType.MESH


def order_table():
    orders = np.arange(ORD)[:, None]
    angles = np.arange(ANGLES)[None, :]
    half = ANGLES // 2
    step = 2.0 * math.pi / ANGLES
    cos = np.cos(step * ((orders * angles) % ANGLES))
    sin = np.sin(step * (((orders - half) * angles) % ANGLES))
    return np.where(orders <= half, cos, sin).astype(np.float32)


def terms(full):
    high = full.astype(BF16)
    low = (full - high.astype(np.float32)).astype(BF16)
    return np.concatenate([high, high, low], axis=1)


def tables():
    table = order_table()
    eye = np.eye(4, dtype=np.float32)
    syn = np.einsum("ka,bc->bakc", table, eye).reshape(BLK, BLK)
    fwd = np.einsum("ka,bc->kbca", table * np.float32(2.0 / ANGLES), eye)
    swap = fwd[np.arange(ORD) ^ 1]
    return (
        terms(syn),
        np.stack([terms(fwd.reshape(BLK, BLK)), terms(swap.reshape(BLK, BLK))]),
    )


def split(value):
    high = value.astype(BF16)
    low = (value - high.astype(F32)).astype(BF16)
    return high, low


def dot(a, b):
    return jnp.dot(a, b, preferred_element_type=F32)


def apply_table(table, one, two):
    high, low = split(jnp.concatenate([one, two], axis=1))
    out = dot(table, jnp.concatenate([high, low, high], axis=0))
    return out[:, :OWN_R], out[:, OWN_R:]


def far_first(n):
    return sorted(range(1, n), key=lambda j: -min(j, n - j))


def kernel(
    pat_hbm, mask_hbm, model_hbm, wig_hbm, syn_hbm, fwd_hbm, out_ref,
    pat, mask, model, wig, syn, fwd,
    pat_t, cyc, logs, score, wig_p, wt, ordt,
    stat, b1, pair, b2, occ1, c1, harm, e1, zsend, e2,
    pat_sem, mask_sem, model_sem, wig_sem, syn_sem, fwd_sem,
    b1_s, b1_r, b2_s, b2_r, c1_s, c1_r, e1_s, e1_r, e2_s, e2_r, known, ring_known,
):
    p_id = lax.axis_index("pat")
    o_id = lax.axis_index("ori")
    x, zl = lax.div(p_id, NZ), lax.rem(p_id, NZ)
    zh, q = lax.div(o_id, NQ), lax.rem(o_id, NQ)
    z = zh * NZ + zl

    def plane_peer(dx, dq):
        return (xs[dx] * NZ + zl, zh * NQ + qs[dq])

    def ring_peer(dz):
        far = lax.rem(z + dz, RING)
        return (x * NZ + lax.rem(far, NZ), lax.div(far, NZ) * NQ + q)

    def pat_peer(dx, dz):
        return (xs[dx] * NZ + zls[dz], o_id)

    pat_peers = [(dx, dz) for dz in far_first(NZ) + [0] for dx in (2, 1, 3, 0) if dx or dz]

    def greet(peer):
        pl.semaphore_signal(barrier, inc=1, device_id=peer, device_id_type=MESH)

    def send(src, dst, ssem, rsem, peer):
        pltpu.make_async_remote_copy(
            src_ref=src, dst_ref=dst, send_sem=ssem, recv_sem=rsem,
            device_id=peer, device_id_type=MESH,
        ).start()

    def whole(buf, ssem, rsem, peer):
        return pltpu.make_async_remote_copy(
            src_ref=buf, dst_ref=buf, send_sem=ssem, recv_sem=rsem,
            device_id=peer, device_id_type=MESH,
        )

    loads = [
        pltpu.make_async_copy(*refs)
        for refs in (
            (model_hbm, model, model_sem), (wig_hbm, wig, wig_sem), (syn_hbm, syn, syn_sem),
            (pat_hbm, pat, pat_sem), (fwd_hbm, fwd, fwd_sem), (mask_hbm, mask, mask_sem),
        )
    ]
    model_in, wig_in, syn_in, pat_in, fwd_in, mask_in = loads
    for load in loads:
        load.start()

    barrier = pltpu.get_barrier_semaphore()
    for d in (4, 12, 3, 13, 2, 14, 1, 15):
        greet(ring_peer(d))
    xs = [lax.rem(x + d, NX) for d in range(NX)]
    qs = [lax.rem(q + d, NQ) for d in range(NQ)]
    zls = [lax.rem(zl + d, NZ) for d in range(NZ)]
    for dx in far_first(NX):
        greet(plane_peer(dx, 0))
    for j in far_first(NQ):
        greet(plane_peer(0, j))

    row = lax.broadcasted_iota(jnp.int32, (16, 128), 0)
    lane = lax.broadcasted_iota(jnp.int32, (16, 128), 1)
    own = [
        jnp.where(lax.div(lane, DEG) == lax.div(row, 4) + n, 1.0, 0.0).astype(BF16)
        for n in (0, 4)
    ]
    upper = lax.broadcasted_iota(jnp.int32, (1, 8, 128), 1) < 4
    model_in.wait()
    wig_in.wait()

    def spread(value):
        tile = value.reshape(RADII // 8, 8, 128)
        other = pltpu.roll(tile, 4, 1)
        one = jnp.where(upper, tile, other)
        two = jnp.where(upper, other, tile)
        rows = []
        for i in range(RADII // 8):
            for half in (one[i], two[i]):
                packed = jnp.concatenate([half, half], axis=0).astype(BF16)
                rows += [packed * own[0], packed * own[1]]
        return jnp.concatenate(rows, axis=0)

    def gather_cycles(g):
        cols = pl.ds(pl.multiple_of(g * 128, 128), 128)
        m = model[:, cols]
        high = m.astype(BF16).astype(F32)
        left = jnp.concatenate([spread(high), spread(m - high)], axis=1)
        w = wig[:, cols]
        out = lax.dot_general(
            left, jnp.concatenate([w, w], axis=1), (((1,), (1,)), ((), ())),
            preferred_element_type=F32,
        )
        cyc[:, pl.ds(pl.multiple_of(g * 32, 32), 32), :] = out.reshape(NBLK, 32, OWN_R)

    @pl.loop(0, 2)
    def _(h):
        for n in range(ORD // 16):
            gather_cycles(h * (ORD // 16) + n)

    syn_in.wait()

    def expand(h, total):
        for m in range(0, NBLK // 2, 2):
            j = h * (NBLK // 2) + m
            for n, part in enumerate(apply_table(syn[...], cyc[j], cyc[j + 1])):
                value = (BACKGROUND + part).astype(BF16)
                logs[pl.ds(pl.multiple_of((j + n) * BLK, BLK), BLK), :] = value
                e = jnp.exp(value.astype(F32))
                total = total + jnp.sum(e.reshape(BLK // 8, 8, OWN_R), axis=0)
        return total

    total = lax.fori_loop(0, 2, expand, jnp.zeros((8, OWN_R), F32))
    intensity = jnp.sum(total, axis=0, keepdims=True)

    pat_in.wait()
    scaled = TEMPER * (dot(pat[...], logs[...]) - intensity)
    for t in range(PT):
        score[t] = scaled[t * 128:(t + 1) * 128, :].T
    peaks, masses = [], []
    for t in range(PT):
        s = score[t]
        m = jnp.max(s, axis=0, keepdims=True)
        peaks.append(m)
        masses.append(jnp.sum(jnp.exp(s - m), axis=0, keepdims=True))
    blank = jnp.zeros((8 - 2 * PT, 128), F32)
    stat[...] = jnp.concatenate(peaks + masses + [blank], axis=0)

    pl.semaphore_wait(barrier, 8 + NX - 1 + NQ - 1)
    for d in (4, 12):
        pl.semaphore_signal(ring_known, inc=1, device_id=ring_peer(d), device_id_type=MESH)

    for j in far_first(NQ):
        send(stat, b1.at[j - 1], b1_s, b1_r, plane_peer(0, j))

    fwd_in.wait()
    mask_in.wait()
    low_half = lax.broadcasted_iota(jnp.int32, (OWN_R, 128), 1) < 64
    for t in range(NQ // 2):
        a = wig[:, t * 128:(t + 1) * 128].astype(F32)
        b = wig[:, 512 + t * 128:512 + (t + 1) * 128].astype(F32)
        wig_p[2 * t] = jnp.where(low_half, a, pltpu.roll(b, 64, 1)).astype(BF16)
        wig_p[2 * t + 1] = jnp.where(low_half, pltpu.roll(a, 64, 1), b).astype(BF16)

    b1_all = whole(b1, b1_s, b1_r, plane_peer(0, 1))
    b1_all.wait_recv()
    peak = stat[0:PT, :]
    for j in range(NQ - 1):
        peak = jnp.maximum(peak, b1[j, 0:PT, :])
    mass = stat[PT:2 * PT, :] * jnp.exp(stat[0:PT, :] - peak)
    for j in range(NQ - 1):
        mass = mass + b1[j, PT:2 * PT, :] * jnp.exp(b1[j, 0:PT, :] - peak)
    pair[...] = jnp.concatenate([peak, mass, blank], axis=0)
    pl.semaphore_wait(ring_known, 2)
    send(pair, b2, b2_s, b2_r, (p_id, (1 - zh) * NQ + q))

    for dx in far_first(NX):
        pl.semaphore_signal(known, inc=1, device_id=plane_peer(dx, 0), device_id_type=MESH)
    zs = [lax.rem(z + d, RING) for d in range(RING)]

    @pl.loop(0, PIX // 128)
    def _(j):
        span = pl.ds(pl.multiple_of(j * 128, 128), 128)
        pat_t[span, :] = pat[:, span].T

    b2_all = whole(b2, b2_s, b2_r, (p_id, (1 - zh) * NQ + q))
    b2_all.wait_recv()
    far_peak = b2[0:PT, :]
    top = jnp.maximum(peak, far_peak)
    mass = mass * jnp.exp(peak - top) + b2[PT:2 * PT, :] * jnp.exp(far_peak - top)
    part = jnp.zeros((8, OWN_R), F32)
    for t in range(PT):
        counts = mask[t * 128:(t + 1) * 128].astype(F32).reshape(1, 128)
        factor = counts / mass[t:t + 1, :]
        w = (jnp.exp(score[t] - top[t:t + 1, :]) * factor).T.astype(BF16)
        wt[t * 128:(t + 1) * 128, :] = w
        part = part + jnp.sum(w.astype(F32).reshape(16, 8, OWN_R), axis=0)
    occ1[...] = jnp.sum(part, axis=0, keepdims=True)

    pl.semaphore_wait(known, NX - 1)
    for dx, dz in pat_peers:
        send(occ1, c1.at[dx * NZ + dz - 1], c1_s, c1_r, pat_peer(dx, dz))

    def compress(i, carry):
        sums = []
        for n in range(4):
            first = n // 2 + 8 * (n % 2)
            rows = [
                pat_t[pl.ds(pl.multiple_of((16 * i + first + 2 * m) * ANGLES, ANGLES), ANGLES), :]
                for m in range(4)
            ]
            sums.append(dot(jnp.concatenate(rows, axis=0), wt[...]))
        evens = apply_table(fwd[0], sums[0], sums[2])
        odds = apply_table(fwd[1], sums[1], sums[3])
        one, two = (
            [v.reshape(ORD // 2, 8, OWN_R) for v in side] for side in (evens, odds)
        )
        cols = pl.ds(pl.multiple_of(i * 16, 16), 16)
        for par in range(2):
            whole_tile = jnp.concatenate(
                [jnp.where(upper, *((a, b) if par == 0 else (b, a))) for a, b in zip(one, two)],
                axis=1,
            )
            for h in range(NH):
                half = whole_tile[h * (ORD // 4):(h + 1) * (ORD // 4)]
                ordt[:, par, cols, h * OWN_R:(h + 1) * OWN_R] = half.astype(BF16)
        return carry

    lax.fori_loop(0, NBLK // 4, compress, 0)
    c1_all = whole(c1, c1_s, c1_r, pat_peer(1, 0))
    c1_all.wait_recv()
    occ = occ1[...] + jnp.sum(c1[...], axis=0)
    inv = (1.0 / math.sqrt(ORIENTS)) / (occ + 1.0)

    slot = lax.rem(lax.div(lax.broadcasted_iota(jnp.int32, (RADII, 128), 1), DEG), 4)

    inv_rows = jnp.broadcast_to(inv, (OWN_R, OWN_R)).T

    def project(i):
        g = qs[i]
        w = wig_p[g].astype(F32) * inv_rows
        both = jnp.concatenate([jnp.where(low_half, w, 0.0), jnp.where(low_half, 0.0, w)], axis=0)
        return dot(ordt[pl.ds(g * 2, 2)].reshape(BLK, 2 * OWN_R), both.astype(BF16))

    def share(i, out):
        g = qs[i]
        acc = [jnp.zeros((RADII, 128), F32)] * 2
        for kk in range(4):
            acc[kk % 2] = jnp.where(slot == kk, out[kk * RADII:(kk + 1) * RADII, :], acc[kk % 2])
        odd = pltpu.roll(acc[1].reshape(RADII // 8, 8, 128), 4, 1).reshape(RADII, 128)
        harm[g] = (acc[0] + odd).astype(BF16).reshape(NX, 16, 128)
        for dx in (2, 1, 3, 0):
            if dx or i:
                send(
                    harm.at[g, xs[dx]], e1.at[dx * NQ + i - 1], e1_s, e1_r,
                    plane_peer(dx, i),
                )

    order = far_first(NQ) + [0]
    ready = [project(order[0])]
    for n, i in enumerate(order):
        ready += [project(later) for later in order[len(ready):n + (3 if n else 2)]]
        share(i, ready[n])
    e1_all = whole(e1, e1_s, e1_r, plane_peer(1, 0))
    e1_all.wait_recv()
    tot = harm[q, x].astype(F32)
    for j in range(PLANE - 1):
        tot = tot + e1[j].astype(F32)
    even, odd = tot[:8], tot[8:]
    first = lane[:8] < 64
    rows = jnp.concatenate(
        [
            jnp.where(first, even, pltpu.roll(odd, 64, 1)),
            jnp.where(first, pltpu.roll(even, 64, 1), odd),
        ],
        axis=0,
    )
    for j in range(RING):
        zsend[j] = rows[j:j + 1, :]
    for j in far_first(RING):
        send(zsend.at[zs[j]], e2.at[j - 1], e2_s, e2_r, ring_peer(j))
    e2_all = whole(e2, e2_s, e2_r, ring_peer(1))
    e2_all.wait_recv()
    fin = zsend[z]
    for j in range(RING - 1):
        fin = fin + e2[j]
    out_ref[0:1, :] = fin[:, :64]
    out_ref[1:2, :] = fin[:, 64:]
    for copies in (b1_all, c1_all, e1_all, e2_all):
        copies.wait_send()
    pltpu.make_async_remote_copy(
        src_ref=pair, dst_ref=b2, send_sem=b2_s, recv_sem=b2_r,
        device_id=(p_id, (1 - zh) * NQ + q), device_id_type=MESH,
    ).wait_send()


def local(patterns, mask, model, wigner):
    syn, fwd = tables()
    hbm = pl.BlockSpec(memory_space=pltpu.MemorySpace.HBM)

    def in_hbm(value):
        return pltpu.with_memory_space_constraint(value, pltpu.MemorySpace.HBM)

    dma = pltpu.SemaphoreType.DMA
    out = pl.pallas_call(
        kernel,
        out_shape=jax.ShapeDtypeStruct((2, 64), F32),
        in_specs=[hbm] * 6,
        out_specs=pl.BlockSpec(memory_space=pltpu.VMEM),
        scratch_shapes=[
            pltpu.VMEM((OWN_P, PIX), BF16),
            pltpu.VMEM((OWN_P,), jnp.int32),
            pltpu.VMEM((RADII, HARM), F32),
            pltpu.VMEM((OWN_R, HARM), BF16),
            pltpu.VMEM(syn.shape, BF16),
            pltpu.VMEM(fwd.shape, BF16),
            pltpu.VMEM((PIX, OWN_P), BF16),
            pltpu.VMEM((NBLK, BLK, OWN_R), F32),
            pltpu.VMEM((PIX, OWN_R), BF16),
            pltpu.VMEM((PT, OWN_R, 128), F32),
            pltpu.VMEM((NQ, OWN_R, 128), BF16),
            pltpu.VMEM((OWN_P, OWN_R), BF16),
            pltpu.VMEM((ORD // 4, 2, RADII, 2 * OWN_R), BF16),
            pltpu.VMEM((8, 128), F32),
            pltpu.VMEM((NQ - 1, 8, 128), F32),
            pltpu.VMEM((8, 128), F32),
            pltpu.VMEM((8, 128), F32),
            pltpu.VMEM((1, 128), F32),
            pltpu.VMEM((NX * NZ - 1, 1, 128), F32),
            pltpu.VMEM((NQ, NX, 16, 128), BF16),
            pltpu.VMEM((PLANE - 1, 16, 128), BF16),
            pltpu.VMEM((RING, 1, 128), F32),
            pltpu.VMEM((RING - 1, 1, 128), F32),
        ]
        + [dma(())] * 16
        + [pltpu.SemaphoreType.REGULAR] * 2,
        compiler_params=pltpu.CompilerParams(
            collective_id=0, has_side_effects=True, vmem_limit_bytes=40 * 1024 * 1024
        ),
        name="recover",
    )(*(in_hbm(v) for v in (patterns, mask, model.T, wigner, jnp.asarray(syn), jnp.asarray(fwd))))
    return out.T


def solution(mesh):
    return jax.shard_map(
        local,
        mesh=mesh,
        in_specs=(P("pat", None), P("pat"), P(), P("ori", None)),
        out_specs=P("ori", "pat"),
        check_vma=False,
    )
```

```python
import math

import jax
import jax.numpy as jnp
import numpy as np
from jax import lax
from jax.experimental import pallas as pl
from jax.experimental.pallas import tpu as pltpu
from jax.sharding import PartitionSpec as P

RADII = 64
ANGLES = 64
DEG = 16
ORD = 64
PIX = 4096
HARM = 1024
PATTERNS = 12288
ORIENTS = 2048

TEMPER = 0.05
BACKGROUND = 0.1

NX, NZ = 4, 8
NH, NQ = 2, 8
PLANE = NX * NQ
RING = NH * NZ
OWN_P = PATTERNS // (NX * NZ)
OWN_R = ORIENTS // (NH * NQ)
PT = OWN_P // 128
BLK = 4 * ANGLES
NBLK = PIX // BLK

F32 = jnp.float32
BF16 = jnp.bfloat16
MESH = pl.DeviceIdType.MESH


def order_table():
    orders = np.arange(ORD)[:, None]
    angles = np.arange(ANGLES)[None, :]
    half = ANGLES // 2
    step = 2.0 * math.pi / ANGLES
    cos = np.cos(step * ((orders * angles) % ANGLES))
    sin = np.sin(step * (((orders - half) * angles) % ANGLES))
    return np.where(orders <= half, cos, sin).astype(np.float32)


def terms(full):
    high = full.astype(BF16)
    low = (full - high.astype(np.float32)).astype(BF16)
    return np.concatenate([high, high, low], axis=1)


def tables():
    table = order_table()
    eye = np.eye(4, dtype=np.float32)
    syn = np.einsum("ka,bc->bakc", table, eye).reshape(BLK, BLK)
    fwd = np.einsum("ka,bc->kbca", table * np.float32(2.0 / ANGLES), eye)
    swap = fwd[np.arange(ORD) ^ 1]
    return (
        terms(syn),
        np.stack([terms(fwd.reshape(BLK, BLK)), terms(swap.reshape(BLK, BLK))]),
    )


def split(value):
    high = value.astype(BF16)
    low = (value - high.astype(F32)).astype(BF16)
    return high, low


def dot(a, b):
    return jnp.dot(a, b, preferred_element_type=F32)


def apply_table(table, one, two):
    high, low = split(jnp.concatenate([one, two], axis=1))
    out = dot(table, jnp.concatenate([high, low, high], axis=0))
    return out[:, :OWN_R], out[:, OWN_R:]


def far_first(n):
    return sorted(range(1, n), key=lambda j: -min(j, n - j))


def kernel(
    pat_hbm, mask_hbm, model_hbm, wig_hbm, syn_hbm, fwd_hbm, out_ref,
    pat, mask, model, wig, syn, fwd,
    pat_t, cyc, logs, score, wig_p, wt, ordt,
    stat, b1, pair, b2, occ1, c1, harm, e1, zsend, e2,
    pat_sem, mask_sem, model_sem, wig_sem, syn_sem, fwd_sem,
    b1_s, b1_r, b2_s, b2_r, c1_s, c1_r, e1_s, e1_r, e2_s, e2_r, known, ring_known,
):
    p_id = lax.axis_index("pat")
    o_id = lax.axis_index("ori")
    x, zl = lax.div(p_id, NZ), lax.rem(p_id, NZ)
    zh, q = lax.div(o_id, NQ), lax.rem(o_id, NQ)
    z = zh * NZ + zl

    def plane_peer(dx, dq):
        return (xs[dx] * NZ + zl, zh * NQ + qs[dq])

    def ring_peer(dz):
        far = lax.rem(z + dz, RING)
        return (x * NZ + lax.rem(far, NZ), lax.div(far, NZ) * NQ + q)

    def pat_peer(dx, dz):
        return (xs[dx] * NZ + zls[dz], o_id)

    pat_peers = [(dx, dz) for dz in far_first(NZ) + [0] for dx in (2, 1, 3, 0) if dx or dz]

    def greet(peer):
        pl.semaphore_signal(barrier, inc=1, device_id=peer, device_id_type=MESH)

    def send(src, dst, ssem, rsem, peer):
        pltpu.make_async_remote_copy(
            src_ref=src, dst_ref=dst, send_sem=ssem, recv_sem=rsem,
            device_id=peer, device_id_type=MESH,
        ).start()

    def whole(buf, ssem, rsem, peer):
        return pltpu.make_async_remote_copy(
            src_ref=buf, dst_ref=buf, send_sem=ssem, recv_sem=rsem,
            device_id=peer, device_id_type=MESH,
        )

    loads = [
        pltpu.make_async_copy(*refs)
        for refs in (
            (model_hbm, model, model_sem), (wig_hbm, wig, wig_sem), (syn_hbm, syn, syn_sem),
            (pat_hbm, pat, pat_sem), (fwd_hbm, fwd, fwd_sem), (mask_hbm, mask, mask_sem),
        )
    ]
    model_in, wig_in, syn_in, pat_in, fwd_in, mask_in = loads
    for load in loads:
        load.start()

    barrier = pltpu.get_barrier_semaphore()
    for d in (4, 12, 3, 13, 2, 14, 1, 15):
        greet(ring_peer(d))
    xs = [lax.rem(x + d, NX) for d in range(NX)]
    qs = [lax.rem(q + d, NQ) for d in range(NQ)]
    zls = [lax.rem(zl + d, NZ) for d in range(NZ)]
    for dx in far_first(NX):
        greet(plane_peer(dx, 0))
    for j in far_first(NQ):
        greet(plane_peer(0, j))

    row = lax.broadcasted_iota(jnp.int32, (16, 128), 0)
    lane = lax.broadcasted_iota(jnp.int32, (16, 128), 1)
    own = [
        jnp.where(lax.div(lane, DEG) == lax.div(row, 4) + n, 1.0, 0.0).astype(BF16)
        for n in (0, 4)
    ]
    upper = lax.broadcasted_iota(jnp.int32, (1, 8, 128), 1) < 4
    model_in.wait()
    wig_in.wait()

    def spread(value):
        tile = value.reshape(RADII // 8, 8, 128)
        other = pltpu.roll(tile, 4, 1)
        one = jnp.where(upper, tile, other)
        two = jnp.where(upper, other, tile)
        rows = []
        for i in range(RADII // 8):
            for half in (one[i], two[i]):
                packed = jnp.concatenate([half, half], axis=0).astype(BF16)
                rows += [packed * own[0], packed * own[1]]
        return jnp.concatenate(rows, axis=0)

    def gather_cycles(g):
        cols = pl.ds(pl.multiple_of(g * 128, 128), 128)
        m = model[:, cols]
        high = m.astype(BF16).astype(F32)
        left = jnp.concatenate([spread(high), spread(m - high)], axis=1)
        w = wig[:, cols]
        out = lax.dot_general(
            left, jnp.concatenate([w, w], axis=1), (((1,), (1,)), ((), ())),
            preferred_element_type=F32,
        )
        cyc[:, pl.ds(pl.multiple_of(g * 32, 32), 32), :] = out.reshape(NBLK, 32, OWN_R)

    for g in range(ORD // 8):
        gather_cycles(g)

    syn_in.wait()

    def expand(h, total):
        for m in range(0, NBLK // 2, 2):
            j = h * (NBLK // 2) + m
            for n, part in enumerate(apply_table(syn[...], cyc[j], cyc[j + 1])):
                value = (BACKGROUND + part).astype(BF16)
                logs[pl.ds(pl.multiple_of((j + n) * BLK, BLK), BLK), :] = value
                e = jnp.exp(value.astype(F32))
                total = total + jnp.sum(e.reshape(BLK // 8, 8, OWN_R), axis=0)
        return total

    total = lax.fori_loop(0, 2, expand, jnp.zeros((8, OWN_R), F32))
    intensity = jnp.sum(total, axis=0, keepdims=True)

    pl.semaphore_wait(barrier, 8 + NX - 1 + NQ - 1)
    for d in (4, 12):
        pl.semaphore_signal(ring_known, inc=1, device_id=ring_peer(d), device_id_type=MESH)

    pat_in.wait()
    scaled = TEMPER * (dot(pat[...], logs[...]) - intensity)
    for t in range(PT):
        score[t] = scaled[t * 128:(t + 1) * 128, :].T
    peaks, masses = [], []
    for t in range(PT):
        s = score[t]
        m = jnp.max(s, axis=0, keepdims=True)
        peaks.append(m)
        masses.append(jnp.sum(jnp.exp(s - m), axis=0, keepdims=True))
    blank = jnp.zeros((8 - 2 * PT, 128), F32)
    stat[...] = jnp.concatenate(peaks + masses + [blank], axis=0)

    for j in far_first(NQ):
        send(stat, b1.at[j - 1], b1_s, b1_r, plane_peer(0, j))

    fwd_in.wait()
    mask_in.wait()
    low_half = lax.broadcasted_iota(jnp.int32, (OWN_R, 128), 1) < 64
    for t in range(NQ // 2):
        a = wig[:, t * 128:(t + 1) * 128].astype(F32)
        b = wig[:, 512 + t * 128:512 + (t + 1) * 128].astype(F32)
        wig_p[2 * t] = jnp.where(low_half, a, pltpu.roll(b, 64, 1)).astype(BF16)
        wig_p[2 * t + 1] = jnp.where(low_half, pltpu.roll(a, 64, 1), b).astype(BF16)

    b1_all = whole(b1, b1_s, b1_r, plane_peer(0, 1))
    b1_all.wait_recv()
    peak = stat[0:PT, :]
    for j in range(NQ - 1):
        peak = jnp.maximum(peak, b1[j, 0:PT, :])
    mass = stat[PT:2 * PT, :] * jnp.exp(stat[0:PT, :] - peak)
    for j in range(NQ - 1):
        mass = mass + b1[j, PT:2 * PT, :] * jnp.exp(b1[j, 0:PT, :] - peak)
    pair[...] = jnp.concatenate([peak, mass, blank], axis=0)
    pl.semaphore_wait(ring_known, 2)
    send(pair, b2, b2_s, b2_r, (p_id, (1 - zh) * NQ + q))

    for dx in far_first(NX):
        pl.semaphore_signal(known, inc=1, device_id=plane_peer(dx, 0), device_id_type=MESH)
    zs = [lax.rem(z + d, RING) for d in range(RING)]

    @pl.loop(0, PIX // 128)
    def _(j):
        span = pl.ds(pl.multiple_of(j * 128, 128), 128)
        pat_t[span, :] = pat[:, span].T

    b2_all = whole(b2, b2_s, b2_r, (p_id, (1 - zh) * NQ + q))
    b2_all.wait_recv()
    far_peak = b2[0:PT, :]
    top = jnp.maximum(peak, far_peak)
    mass = mass * jnp.exp(peak - top) + b2[PT:2 * PT, :] * jnp.exp(far_peak - top)
    part = jnp.zeros((8, OWN_R), F32)
    for t in range(PT):
        counts = mask[t * 128:(t + 1) * 128].astype(F32).reshape(1, 128)
        factor = counts / mass[t:t + 1, :]
        w = (jnp.exp(score[t] - top[t:t + 1, :]) * factor).T.astype(BF16)
        wt[t * 128:(t + 1) * 128, :] = w
        part = part + jnp.sum(w.astype(F32).reshape(16, 8, OWN_R), axis=0)
    occ1[...] = jnp.sum(part, axis=0, keepdims=True)

    pl.semaphore_wait(known, NX - 1)
    for dx, dz in pat_peers:
        send(occ1, c1.at[dx * NZ + dz - 1], c1_s, c1_r, pat_peer(dx, dz))

    def compress(i, carry):
        sums = []
        for n in range(4):
            first = n // 2 + 8 * (n % 2)
            rows = [
                pat_t[pl.ds(pl.multiple_of((16 * i + first + 2 * m) * ANGLES, ANGLES), ANGLES), :]
                for m in range(4)
            ]
            sums.append(dot(jnp.concatenate(rows, axis=0), wt[...]))
        evens = apply_table(fwd[0], sums[0], sums[2])
        odds = apply_table(fwd[1], sums[1], sums[3])
        one, two = (
            [v.reshape(ORD // 2, 8, OWN_R) for v in side] for side in (evens, odds)
        )
        cols = pl.ds(pl.multiple_of(i * 16, 16), 16)
        for par in range(2):
            whole_tile = jnp.concatenate(
                [jnp.where(upper, *((a, b) if par == 0 else (b, a))) for a, b in zip(one, two)],
                axis=1,
            )
            for h in range(NH):
                half = whole_tile[h * (ORD // 4):(h + 1) * (ORD // 4)]
                ordt[:, par, cols, h * OWN_R:(h + 1) * OWN_R] = half.astype(BF16)
        return carry

    lax.fori_loop(0, NBLK // 4, compress, 0)
    c1_all = whole(c1, c1_s, c1_r, pat_peer(1, 0))
    c1_all.wait_recv()
    occ = occ1[...] + jnp.sum(c1[...], axis=0)
    inv = (1.0 / math.sqrt(ORIENTS)) / (occ + 1.0)

    slot = lax.rem(lax.div(lax.broadcasted_iota(jnp.int32, (RADII, 128), 1), DEG), 4)

    inv_rows = jnp.broadcast_to(inv, (OWN_R, OWN_R)).T

    def project(i):
        g = qs[i]
        w = wig_p[g].astype(F32) * inv_rows
        both = jnp.concatenate([jnp.where(low_half, w, 0.0), jnp.where(low_half, 0.0, w)], axis=0)
        return dot(ordt[pl.ds(g * 2, 2)].reshape(BLK, 2 * OWN_R), both.astype(BF16))

    def share(i, out):
        g = qs[i]
        acc = [jnp.zeros((RADII, 128), F32)] * 2
        for kk in range(4):
            acc[kk % 2] = jnp.where(slot == kk, out[kk * RADII:(kk + 1) * RADII, :], acc[kk % 2])
        odd = pltpu.roll(acc[1].reshape(RADII // 8, 8, 128), 4, 1).reshape(RADII, 128)
        harm[g] = (acc[0] + odd).astype(BF16).reshape(NX, 16, 128)
        for dx in (2, 1, 3, 0):
            if dx or i:
                send(
                    harm.at[g, xs[dx]], e1.at[dx * NQ + i - 1], e1_s, e1_r,
                    plane_peer(dx, i),
                )

    order = far_first(NQ) + [0]
    ready = [project(order[0])]
    for n, i in enumerate(order):
        ready += [project(later) for later in order[len(ready):n + (3 if n else 2)]]
        share(i, ready[n])
    e1_all = whole(e1, e1_s, e1_r, plane_peer(1, 0))
    e1_all.wait_recv()
    tot = harm[q, x].astype(F32)
    for j in range(PLANE - 1):
        tot = tot + e1[j].astype(F32)
    even, odd = tot[:8], tot[8:]
    first = lane[:8] < 64
    rows = jnp.concatenate(
        [
            jnp.where(first, even, pltpu.roll(odd, 64, 1)),
            jnp.where(first, pltpu.roll(even, 64, 1), odd),
        ],
        axis=0,
    )
    for j in range(RING):
        zsend[j] = rows[j:j + 1, :]
    for j in far_first(RING):
        send(zsend.at[zs[j]], e2.at[j - 1], e2_s, e2_r, ring_peer(j))
    e2_all = whole(e2, e2_s, e2_r, ring_peer(1))
    e2_all.wait_recv()
    fin = zsend[z]
    for j in range(RING - 1):
        fin = fin + e2[j]
    out_ref[0:1, :] = fin[:, :64]
    out_ref[1:2, :] = fin[:, 64:]
    for copies in (b1_all, c1_all, e1_all, e2_all):
        copies.wait_send()
    pltpu.make_async_remote_copy(
        src_ref=pair, dst_ref=b2, send_sem=b2_s, recv_sem=b2_r,
        device_id=(p_id, (1 - zh) * NQ + q), device_id_type=MESH,
    ).wait_send()


def local(patterns, mask, model, wigner):
    syn, fwd = tables()
    hbm = pl.BlockSpec(memory_space=pltpu.MemorySpace.HBM)

    def in_hbm(value):
        return pltpu.with_memory_space_constraint(value, pltpu.MemorySpace.HBM)

    dma = pltpu.SemaphoreType.DMA
    out = pl.pallas_call(
        kernel,
        out_shape=jax.ShapeDtypeStruct((2, 64), F32),
        in_specs=[hbm] * 6,
        out_specs=pl.BlockSpec(memory_space=pltpu.VMEM),
        scratch_shapes=[
            pltpu.VMEM((OWN_P, PIX), BF16),
            pltpu.VMEM((OWN_P,), jnp.int32),
            pltpu.VMEM((RADII, HARM), F32),
            pltpu.VMEM((OWN_R, HARM), BF16),
            pltpu.VMEM(syn.shape, BF16),
            pltpu.VMEM(fwd.shape, BF16),
            pltpu.VMEM((PIX, OWN_P), BF16),
            pltpu.VMEM((NBLK, BLK, OWN_R), F32),
            pltpu.VMEM((PIX, OWN_R), BF16),
            pltpu.VMEM((PT, OWN_R, 128), F32),
            pltpu.VMEM((NQ, OWN_R, 128), BF16),
            pltpu.VMEM((OWN_P, OWN_R), BF16),
            pltpu.VMEM((ORD // 4, 2, RADII, 2 * OWN_R), BF16),
            pltpu.VMEM((8, 128), F32),
            pltpu.VMEM((NQ - 1, 8, 128), F32),
            pltpu.VMEM((8, 128), F32),
            pltpu.VMEM((8, 128), F32),
            pltpu.VMEM((1, 128), F32),
            pltpu.VMEM((NX * NZ - 1, 1, 128), F32),
            pltpu.VMEM((NQ, NX, 16, 128), BF16),
            pltpu.VMEM((PLANE - 1, 16, 128), BF16),
            pltpu.VMEM((RING, 1, 128), F32),
            pltpu.VMEM((RING - 1, 1, 128), F32),
        ]
        + [dma(())] * 16
        + [pltpu.SemaphoreType.REGULAR] * 2,
        compiler_params=pltpu.CompilerParams(
            collective_id=0, has_side_effects=True, vmem_limit_bytes=40 * 1024 * 1024
        ),
        name="recover",
    )(*(in_hbm(v) for v in (patterns, mask, model.T, wigner, jnp.asarray(syn), jnp.asarray(fwd))))
    return out.T


def solution(mesh):
    return jax.shard_map(
        local,
        mesh=mesh,
        in_specs=(P("pat", None), P("pat"), P(), P("ori", None)),
        out_specs=P("ori", "pat"),
        check_vma=False,
    )
```

```python
import math

import jax
import jax.numpy as jnp
import numpy as np
from jax import lax
from jax.experimental import pallas as pl
from jax.experimental.pallas import tpu as pltpu
from jax.sharding import PartitionSpec as P

RADII = 64
ANGLES = 64
DEG = 16
ORD = 64
PIX = 4096
HARM = 1024
PATTERNS = 12288
ORIENTS = 2048

TEMPER = 0.05
BACKGROUND = 0.1

NX, NZ = 4, 8
NH, NQ = 2, 8
PLANE = NX * NQ
RING = NH * NZ
OWN_P = PATTERNS // (NX * NZ)
OWN_R = ORIENTS // (NH * NQ)
PT = OWN_P // 128
BLK = 4 * ANGLES
NBLK = PIX // BLK

F32 = jnp.float32
BF16 = jnp.bfloat16
MESH = pl.DeviceIdType.MESH


def order_table():
    orders = np.arange(ORD)[:, None]
    angles = np.arange(ANGLES)[None, :]
    half = ANGLES // 2
    step = 2.0 * math.pi / ANGLES
    cos = np.cos(step * ((orders * angles) % ANGLES))
    sin = np.sin(step * (((orders - half) * angles) % ANGLES))
    return np.where(orders <= half, cos, sin).astype(np.float32)


def terms(full):
    high = full.astype(BF16)
    low = (full - high.astype(np.float32)).astype(BF16)
    return np.concatenate([high, high, low], axis=1)


def tables():
    table = order_table()
    eye = np.eye(4, dtype=np.float32)
    syn = np.einsum("ka,bc->bakc", table, eye).reshape(BLK, BLK)
    fwd = np.einsum("ka,bc->kbca", table * np.float32(2.0 / ANGLES), eye)
    swap = fwd[np.arange(ORD) ^ 1]
    return (
        terms(syn),
        np.stack([terms(fwd.reshape(BLK, BLK)), terms(swap.reshape(BLK, BLK))]),
    )


def split(value):
    high = value.astype(BF16)
    low = (value - high.astype(F32)).astype(BF16)
    return high, low


def dot(a, b):
    return jnp.dot(a, b, preferred_element_type=F32)


def apply_table(table, one, two):
    high, low = split(jnp.concatenate([one, two], axis=1))
    out = dot(table, jnp.concatenate([high, low, high], axis=0))
    return out[:, :OWN_R], out[:, OWN_R:]


def far_first(n):
    return sorted(range(1, n), key=lambda j: -min(j, n - j))


def kernel(
    pat_hbm, mask_hbm, model_hbm, wig_hbm, syn_hbm, fwd_hbm, out_ref,
    pat, mask, model, wig, syn, fwd,
    pat_t, cyc, logs, score, wig_p, wt, ordt,
    stat, b1, pair, b2, occ1, c1, harm, e1, zsend, e2,
    pat_sem, mask_sem, model_sem, wig_sem, syn_sem, fwd_sem,
    b1_s, b1_r, b2_s, b2_r, c1_s, c1_r, e1_s, e1_r, e2_s, e2_r, known, ring_known,
):
    p_id = lax.axis_index("pat")
    o_id = lax.axis_index("ori")
    x, zl = lax.div(p_id, NZ), lax.rem(p_id, NZ)
    zh, q = lax.div(o_id, NQ), lax.rem(o_id, NQ)
    z = zh * NZ + zl

    def plane_peer(dx, dq):
        return (xs[dx] * NZ + zl, zh * NQ + qs[dq])

    def ring_peer(dz):
        far = lax.rem(z + dz, RING)
        return (x * NZ + lax.rem(far, NZ), lax.div(far, NZ) * NQ + q)

    def pat_peer(dx, dz):
        return (xs[dx] * NZ + zls[dz], o_id)


    def greet(peer):
        pl.semaphore_signal(barrier, inc=1, device_id=peer, device_id_type=MESH)

    def send(src, dst, ssem, rsem, peer):
        pltpu.make_async_remote_copy(
            src_ref=src, dst_ref=dst, send_sem=ssem, recv_sem=rsem,
            device_id=peer, device_id_type=MESH,
        ).start()

    def whole(buf, ssem, rsem, peer):
        return pltpu.make_async_remote_copy(
            src_ref=buf, dst_ref=buf, send_sem=ssem, recv_sem=rsem,
            device_id=peer, device_id_type=MESH,
        )

    loads = [
        pltpu.make_async_copy(*refs)
        for refs in (
            (model_hbm, model, model_sem), (wig_hbm, wig, wig_sem), (syn_hbm, syn, syn_sem),
            (pat_hbm, pat, pat_sem), (fwd_hbm, fwd, fwd_sem), (mask_hbm, mask, mask_sem),
        )
    ]
    model_in, wig_in, syn_in, pat_in, fwd_in, mask_in = loads
    for load in loads:
        load.start()

    barrier = pltpu.get_barrier_semaphore()
    for d in (4, 12, 3, 13, 2, 14, 1, 15):
        greet(ring_peer(d))
    xs = [lax.rem(x + d, NX) for d in range(NX)]
    qs = [lax.rem(q + d, NQ) for d in range(NQ)]
    zls = [lax.rem(zl + d, NZ) for d in range(NZ)]
    for dx in far_first(NX):
        greet(plane_peer(dx, 0))
    for j in far_first(NQ):
        greet(plane_peer(0, j))

    row = lax.broadcasted_iota(jnp.int32, (16, 128), 0)
    lane = lax.broadcasted_iota(jnp.int32, (16, 128), 1)
    own = [
        jnp.where(lax.div(lane, DEG) == lax.div(row, 4) + n, 1.0, 0.0).astype(BF16)
        for n in (0, 4)
    ]
    upper = lax.broadcasted_iota(jnp.int32, (1, 8, 128), 1) < 4
    model_in.wait()
    wig_in.wait()

    def spread(value):
        tile = value.reshape(RADII // 8, 8, 128)
        other = pltpu.roll(tile, 4, 1)
        one = jnp.where(upper, tile, other)
        two = jnp.where(upper, other, tile)
        rows = []
        for i in range(RADII // 8):
            for half in (one[i], two[i]):
                packed = jnp.concatenate([half, half], axis=0).astype(BF16)
                rows += [packed * own[0], packed * own[1]]
        return jnp.concatenate(rows, axis=0)

    def gather_cycles(g):
        cols = pl.ds(pl.multiple_of(g * 128, 128), 128)
        m = model[:, cols]
        high = m.astype(BF16).astype(F32)
        left = jnp.concatenate([spread(high), spread(m - high)], axis=1)
        w = wig[:, cols]
        out = lax.dot_general(
            left, jnp.concatenate([w, w], axis=1), (((1,), (1,)), ((), ())),
            preferred_element_type=F32,
        )
        cyc[:, pl.ds(pl.multiple_of(g * 32, 32), 32), :] = out.reshape(NBLK, 32, OWN_R)

    for g in range(ORD // 8):
        gather_cycles(g)

    syn_in.wait()

    def expand(h, total):
        for m in range(0, NBLK // 2, 2):
            j = h * (NBLK // 2) + m
            for n, part in enumerate(apply_table(syn[...], cyc[j], cyc[j + 1])):
                value = (BACKGROUND + part).astype(BF16)
                logs[pl.ds(pl.multiple_of((j + n) * BLK, BLK), BLK), :] = value
                e = jnp.exp(value.astype(F32))
                total = total + jnp.sum(e.reshape(BLK // 8, 8, OWN_R), axis=0)
        return total

    total = lax.fori_loop(0, 2, expand, jnp.zeros((8, OWN_R), F32))
    intensity = jnp.sum(total, axis=0, keepdims=True)

    pl.semaphore_wait(barrier, 8 + NX - 1 + NQ - 1)
    for d in (4, 12):
        pl.semaphore_signal(ring_known, inc=1, device_id=ring_peer(d), device_id_type=MESH)

    pat_in.wait()
    scaled = TEMPER * (dot(pat[...], logs[...]) - intensity)
    for t in range(PT):
        score[t] = scaled[t * 128:(t + 1) * 128, :].T
    peaks, masses = [], []
    for t in range(PT):
        s = score[t]
        m = jnp.max(s, axis=0, keepdims=True)
        peaks.append(m)
        masses.append(jnp.sum(jnp.exp(s - m), axis=0, keepdims=True))
    blank = jnp.zeros((8 - 2 * PT, 128), F32)
    stat[...] = jnp.concatenate(peaks + masses + [blank], axis=0)

    for j in far_first(NQ):
        send(stat, b1.at[j - 1], b1_s, b1_r, plane_peer(0, j))

    fwd_in.wait()
    mask_in.wait()
    low_half = lax.broadcasted_iota(jnp.int32, (OWN_R, 128), 1) < 64
    for t in range(NQ // 2):
        a = wig[:, t * 128:(t + 1) * 128].astype(F32)
        b = wig[:, 512 + t * 128:512 + (t + 1) * 128].astype(F32)
        wig_p[2 * t] = jnp.where(low_half, a, pltpu.roll(b, 64, 1)).astype(BF16)
        wig_p[2 * t + 1] = jnp.where(low_half, pltpu.roll(a, 64, 1), b).astype(BF16)

    b1_all = whole(b1, b1_s, b1_r, plane_peer(0, 1))
    b1_all.wait_recv()
    peak = stat[0:PT, :]
    for j in range(NQ - 1):
        peak = jnp.maximum(peak, b1[j, 0:PT, :])
    mass = stat[PT:2 * PT, :] * jnp.exp(stat[0:PT, :] - peak)
    for j in range(NQ - 1):
        mass = mass + b1[j, PT:2 * PT, :] * jnp.exp(b1[j, 0:PT, :] - peak)
    pair[...] = jnp.concatenate([peak, mass, blank], axis=0)
    pl.semaphore_wait(ring_known, 2)
    send(pair, b2, b2_s, b2_r, (p_id, (1 - zh) * NQ + q))

    for dx in far_first(NX):
        pl.semaphore_signal(known, inc=1, device_id=plane_peer(dx, 0), device_id_type=MESH)
    zs = [lax.rem(z + d, RING) for d in range(RING)]

    @pl.loop(0, PIX // 128)
    def _(j):
        span = pl.ds(pl.multiple_of(j * 128, 128), 128)
        pat_t[span, :] = pat[:, span].T

    b2_all = whole(b2, b2_s, b2_r, (p_id, (1 - zh) * NQ + q))
    b2_all.wait_recv()
    far_peak = b2[0:PT, :]
    top = jnp.maximum(peak, far_peak)
    mass = mass * jnp.exp(peak - top) + b2[PT:2 * PT, :] * jnp.exp(far_peak - top)
    part = jnp.zeros((8, OWN_R), F32)
    for t in range(PT):
        counts = mask[t * 128:(t + 1) * 128].astype(F32).reshape(1, 128)
        factor = counts / mass[t:t + 1, :]
        w = (jnp.exp(score[t] - top[t:t + 1, :]) * factor).T.astype(BF16)
        wt[t * 128:(t + 1) * 128, :] = w
        part = part + jnp.sum(w.astype(F32).reshape(16, 8, OWN_R), axis=0)
    occ1[...] = jnp.sum(part, axis=0, keepdims=True)

    pl.semaphore_wait(known, NX - 1)
    high_end = lax.div(zl, NZ // 2)
    for n in range(1, NZ):
        dz = high_end * n + (1 - high_end) * (NZ - n)
        for dx in (2, 1, 3, 0):
            peer = (xs[dx] * NZ + lax.rem(zl + dz, NZ), o_id)
            send(occ1, c1.at[dx * NZ + dz - 1], c1_s, c1_r, peer)
    for dx in far_first(NX):
        send(occ1, c1.at[dx * NZ - 1], c1_s, c1_r, pat_peer(dx, 0))

    def compress(i, carry):
        sums = []
        for n in range(4):
            first = n // 2 + 8 * (n % 2)
            rows = [
                pat_t[pl.ds(pl.multiple_of((16 * i + first + 2 * m) * ANGLES, ANGLES), ANGLES), :]
                for m in range(4)
            ]
            sums.append(dot(jnp.concatenate(rows, axis=0), wt[...]))
        evens = apply_table(fwd[0], sums[0], sums[2])
        odds = apply_table(fwd[1], sums[1], sums[3])
        one, two = (
            [v.reshape(ORD // 2, 8, OWN_R) for v in side] for side in (evens, odds)
        )
        cols = pl.ds(pl.multiple_of(i * 16, 16), 16)
        for par in range(2):
            whole_tile = jnp.concatenate(
                [jnp.where(upper, *((a, b) if par == 0 else (b, a))) for a, b in zip(one, two)],
                axis=1,
            )
            for h in range(NH):
                half = whole_tile[h * (ORD // 4):(h + 1) * (ORD // 4)]
                ordt[:, par, cols, h * OWN_R:(h + 1) * OWN_R] = half.astype(BF16)
        return carry

    lax.fori_loop(0, NBLK // 4, compress, 0)
    c1_all = whole(c1, c1_s, c1_r, pat_peer(1, 0))
    c1_all.wait_recv()
    occ = occ1[...] + jnp.sum(c1[...], axis=0)
    inv = (1.0 / math.sqrt(ORIENTS)) / (occ + 1.0)

    slot = lax.rem(lax.div(lax.broadcasted_iota(jnp.int32, (RADII, 128), 1), DEG), 4)

    inv_rows = jnp.broadcast_to(inv, (OWN_R, OWN_R)).T

    def project(i):
        g = qs[i]
        w = wig_p[g].astype(F32) * inv_rows
        both = jnp.concatenate([jnp.where(low_half, w, 0.0), jnp.where(low_half, 0.0, w)], axis=0)
        return dot(ordt[pl.ds(g * 2, 2)].reshape(BLK, 2 * OWN_R), both.astype(BF16))

    def share(i, out):
        g = qs[i]
        acc = [jnp.zeros((RADII, 128), F32)] * 2
        for kk in range(4):
            acc[kk % 2] = jnp.where(slot == kk, out[kk * RADII:(kk + 1) * RADII, :], acc[kk % 2])
        odd = pltpu.roll(acc[1].reshape(RADII // 8, 8, 128), 4, 1).reshape(RADII, 128)
        harm[g] = (acc[0] + odd).astype(BF16).reshape(NX, 16, 128)
        for dx in (2, 1, 3, 0):
            if dx or i:
                send(
                    harm.at[g, xs[dx]], e1.at[dx * NQ + i - 1], e1_s, e1_r,
                    plane_peer(dx, i),
                )

    order = far_first(NQ) + [0]
    ready = [project(order[0])]
    for n, i in enumerate(order):
        ready += [project(later) for later in order[len(ready):n + (3 if n else 2)]]
        share(i, ready[n])
    e1_all = whole(e1, e1_s, e1_r, plane_peer(1, 0))
    e1_all.wait_recv()
    tot = harm[q, x].astype(F32)
    for j in range(PLANE - 1):
        tot = tot + e1[j].astype(F32)
    even, odd = tot[:8], tot[8:]
    first = lane[:8] < 64
    rows = jnp.concatenate(
        [
            jnp.where(first, even, pltpu.roll(odd, 64, 1)),
            jnp.where(first, pltpu.roll(even, 64, 1), odd),
        ],
        axis=0,
    )
    for j in range(RING):
        zsend[j] = rows[j:j + 1, :]
    for j in far_first(RING):
        send(zsend.at[zs[j]], e2.at[j - 1], e2_s, e2_r, ring_peer(j))
    e2_all = whole(e2, e2_s, e2_r, ring_peer(1))
    e2_all.wait_recv()
    fin = zsend[z]
    for j in range(RING - 1):
        fin = fin + e2[j]
    out_ref[0:1, :] = fin[:, :64]
    out_ref[1:2, :] = fin[:, 64:]
    for copies in (b1_all, c1_all, e1_all, e2_all):
        copies.wait_send()
    pltpu.make_async_remote_copy(
        src_ref=pair, dst_ref=b2, send_sem=b2_s, recv_sem=b2_r,
        device_id=(p_id, (1 - zh) * NQ + q), device_id_type=MESH,
    ).wait_send()


def local(patterns, mask, model, wigner):
    syn, fwd = tables()
    hbm = pl.BlockSpec(memory_space=pltpu.MemorySpace.HBM)

    def in_hbm(value):
        return pltpu.with_memory_space_constraint(value, pltpu.MemorySpace.HBM)

    dma = pltpu.SemaphoreType.DMA
    out = pl.pallas_call(
        kernel,
        out_shape=jax.ShapeDtypeStruct((2, 64), F32),
        in_specs=[hbm] * 6,
        out_specs=pl.BlockSpec(memory_space=pltpu.VMEM),
        scratch_shapes=[
            pltpu.VMEM((OWN_P, PIX), BF16),
            pltpu.VMEM((OWN_P,), jnp.int32),
            pltpu.VMEM((RADII, HARM), F32),
            pltpu.VMEM((OWN_R, HARM), BF16),
            pltpu.VMEM(syn.shape, BF16),
            pltpu.VMEM(fwd.shape, BF16),
            pltpu.VMEM((PIX, OWN_P), BF16),
            pltpu.VMEM((NBLK, BLK, OWN_R), F32),
            pltpu.VMEM((PIX, OWN_R), BF16),
            pltpu.VMEM((PT, OWN_R, 128), F32),
            pltpu.VMEM((NQ, OWN_R, 128), BF16),
            pltpu.VMEM((OWN_P, OWN_R), BF16),
            pltpu.VMEM((ORD // 4, 2, RADII, 2 * OWN_R), BF16),
            pltpu.VMEM((8, 128), F32),
            pltpu.VMEM((NQ - 1, 8, 128), F32),
            pltpu.VMEM((8, 128), F32),
            pltpu.VMEM((8, 128), F32),
            pltpu.VMEM((1, 128), F32),
            pltpu.VMEM((NX * NZ - 1, 1, 128), F32),
            pltpu.VMEM((NQ, NX, 16, 128), BF16),
            pltpu.VMEM((PLANE - 1, 16, 128), BF16),
            pltpu.VMEM((RING, 1, 128), F32),
            pltpu.VMEM((RING - 1, 1, 128), F32),
        ]
        + [dma(())] * 16
        + [pltpu.SemaphoreType.REGULAR] * 2,
        compiler_params=pltpu.CompilerParams(
            collective_id=0, has_side_effects=True, vmem_limit_bytes=40 * 1024 * 1024
        ),
        name="recover",
    )(*(in_hbm(v) for v in (patterns, mask, model.T, wigner, jnp.asarray(syn), jnp.asarray(fwd))))
    return out.T


def solution(mesh):
    return jax.shard_map(
        local,
        mesh=mesh,
        in_specs=(P("pat", None), P("pat"), P(), P("ori", None)),
        out_specs=P("ori", "pat"),
        check_vma=False,
    )
```

```python
import math

import jax
import jax.numpy as jnp
import numpy as np
from jax import lax
from jax.experimental import pallas as pl
from jax.experimental.pallas import tpu as pltpu
from jax.sharding import PartitionSpec as P

RADII = 64
ANGLES = 64
DEG = 16
ORD = 64
PIX = 4096
HARM = 1024
PATTERNS = 12288
ORIENTS = 2048

TEMPER = 0.05
BACKGROUND = 0.1

NX, NZ = 4, 8
NH, NQ = 2, 8
PLANE = NX * NQ
RING = NH * NZ
OWN_P = PATTERNS // (NX * NZ)
OWN_R = ORIENTS // (NH * NQ)
PT = OWN_P // 128
BLK = 4 * ANGLES
NBLK = PIX // BLK

F32 = jnp.float32
BF16 = jnp.bfloat16
MESH = pl.DeviceIdType.MESH


def order_table():
    orders = np.arange(ORD)[:, None]
    angles = np.arange(ANGLES)[None, :]
    half = ANGLES // 2
    step = 2.0 * math.pi / ANGLES
    cos = np.cos(step * ((orders * angles) % ANGLES))
    sin = np.sin(step * (((orders - half) * angles) % ANGLES))
    return np.where(orders <= half, cos, sin).astype(np.float32)


def terms(full):
    high = full.astype(BF16)
    low = (full - high.astype(np.float32)).astype(BF16)
    return np.concatenate([high, high, low], axis=1)


def tables():
    table = order_table()
    eye = np.eye(4, dtype=np.float32)
    syn = np.einsum("ka,bc->bakc", table, eye).reshape(BLK, BLK)
    fwd = np.einsum("ka,bc->kbca", table * np.float32(2.0 / ANGLES), eye)
    swap = fwd[np.arange(ORD) ^ 1]
    return (
        terms(syn),
        np.stack([terms(fwd.reshape(BLK, BLK)), terms(swap.reshape(BLK, BLK))]),
    )


def split(value):
    high = value.astype(BF16)
    low = (value - high.astype(F32)).astype(BF16)
    return high, low


def dot(a, b):
    return jnp.dot(a, b, preferred_element_type=F32)


def apply_table(table, one, two):
    high, low = split(jnp.concatenate([one, two], axis=1))
    out = dot(table, jnp.concatenate([high, low, high], axis=0))
    return out[:, :OWN_R], out[:, OWN_R:]


def far_first(n):
    return sorted(range(1, n), key=lambda j: -min(j, n - j))


def kernel(
    pat_hbm, mask_hbm, model_hbm, wig_hbm, syn_hbm, fwd_hbm, out_ref,
    pat, mask, model, wig, syn, fwd,
    pat_t, cyc, logs, score, wig_p, wt, ordt,
    stat, b1, pair, b2, occ1, c1, harm, e1, zsend, e2,
    pat_sem, mask_sem, model_sem, wig_sem, syn_sem, fwd_sem,
    b1_s, b1_r, b2_s, b2_r, c1_s, c1_r, e1_s, e1_r, e2_s, e2_r, known, ring_known,
):
    p_id = lax.axis_index("pat")
    o_id = lax.axis_index("ori")
    x, zl = lax.div(p_id, NZ), lax.rem(p_id, NZ)
    zh, q = lax.div(o_id, NQ), lax.rem(o_id, NQ)
    z = zh * NZ + zl

    def plane_peer(dx, dq):
        return (xs[dx] * NZ + zl, zh * NQ + qs[dq])

    def ring_peer(dz):
        far = lax.rem(z + dz, RING)
        return (x * NZ + lax.rem(far, NZ), lax.div(far, NZ) * NQ + q)

    def pat_peer(dx, dz):
        return (xs[dx] * NZ + zls[dz], o_id)


    def greet(peer):
        pl.semaphore_signal(barrier, inc=1, device_id=peer, device_id_type=MESH)

    def send(src, dst, ssem, rsem, peer):
        pltpu.make_async_remote_copy(
            src_ref=src, dst_ref=dst, send_sem=ssem, recv_sem=rsem,
            device_id=peer, device_id_type=MESH,
        ).start()

    def whole(buf, ssem, rsem, peer):
        return pltpu.make_async_remote_copy(
            src_ref=buf, dst_ref=buf, send_sem=ssem, recv_sem=rsem,
            device_id=peer, device_id_type=MESH,
        )

    loads = [
        pltpu.make_async_copy(*refs)
        for refs in (
            (model_hbm, model, model_sem), (wig_hbm, wig, wig_sem), (syn_hbm, syn, syn_sem),
            (pat_hbm, pat, pat_sem), (fwd_hbm, fwd, fwd_sem), (mask_hbm, mask, mask_sem),
        )
    ]
    model_in, wig_in, syn_in, pat_in, fwd_in, mask_in = loads
    for load in loads:
        load.start()

    barrier = pltpu.get_barrier_semaphore()
    for d in (4, 12, 3, 13, 2, 14, 1, 15):
        greet(ring_peer(d))
    xs = [lax.rem(x + d, NX) for d in range(NX)]
    qs = [lax.rem(q + d, NQ) for d in range(NQ)]
    zls = [lax.rem(zl + d, NZ) for d in range(NZ)]
    for dx in far_first(NX):
        greet(plane_peer(dx, 0))
    for j in far_first(NQ):
        greet(plane_peer(0, j))

    row = lax.broadcasted_iota(jnp.int32, (16, 128), 0)
    lane = lax.broadcasted_iota(jnp.int32, (16, 128), 1)
    own = [
        jnp.where(lax.div(lane, DEG) == lax.div(row, 4) + n, 1.0, 0.0).astype(BF16)
        for n in (0, 4)
    ]
    upper = lax.broadcasted_iota(jnp.int32, (1, 8, 128), 1) < 4
    model_in.wait()
    wig_in.wait()

    def spread(value):
        tile = value.reshape(RADII // 8, 8, 128)
        other = pltpu.roll(tile, 4, 1)
        one = jnp.where(upper, tile, other)
        two = jnp.where(upper, other, tile)
        rows = []
        for i in range(RADII // 8):
            for half in (one[i], two[i]):
                packed = jnp.concatenate([half, half], axis=0).astype(BF16)
                rows += [packed * own[0], packed * own[1]]
        return jnp.concatenate(rows, axis=0)

    def gather_cycles(g):
        cols = pl.ds(pl.multiple_of(g * 128, 128), 128)
        m = model[:, cols]
        high = m.astype(BF16).astype(F32)
        left = jnp.concatenate([spread(high), spread(m - high)], axis=1)
        w = wig[:, cols]
        out = lax.dot_general(
            left, jnp.concatenate([w, w], axis=1), (((1,), (1,)), ((), ())),
            preferred_element_type=F32,
        )
        cyc[:, pl.ds(pl.multiple_of(g * 32, 32), 32), :] = out.reshape(NBLK, 32, OWN_R)

    for g in range(ORD // 8):
        gather_cycles(g)

    syn_in.wait()

    def expand(h, total):
        for m in range(0, NBLK // 2, 2):
            j = h * (NBLK // 2) + m
            for n, part in enumerate(apply_table(syn[...], cyc[j], cyc[j + 1])):
                value = (BACKGROUND + part).astype(BF16)
                logs[pl.ds(pl.multiple_of((j + n) * BLK, BLK), BLK), :] = value
                e = jnp.exp(value.astype(F32))
                total = total + jnp.sum(e.reshape(BLK // 8, 8, OWN_R), axis=0)
        return total

    total = lax.fori_loop(0, 2, expand, jnp.zeros((8, OWN_R), F32))
    intensity = jnp.sum(total, axis=0, keepdims=True)

    pl.semaphore_wait(barrier, 8 + NX - 1 + NQ - 1)
    for d in (4, 12):
        pl.semaphore_signal(ring_known, inc=1, device_id=ring_peer(d), device_id_type=MESH)

    pat_in.wait()
    scaled = TEMPER * (dot(pat[...], logs[...]) - intensity)
    for t in range(PT):
        score[t] = scaled[t * 128:(t + 1) * 128, :].T
    peaks, masses = [], []
    for t in range(PT):
        s = score[t]
        m = jnp.max(s, axis=0, keepdims=True)
        peaks.append(m)
        masses.append(jnp.sum(jnp.exp(s - m), axis=0, keepdims=True))
    blank = jnp.zeros((8 - 2 * PT, 128), F32)
    stat[...] = jnp.concatenate(peaks + masses + [blank], axis=0)

    for j in far_first(NQ):
        send(stat, b1.at[j - 1], b1_s, b1_r, plane_peer(0, j))

    fwd_in.wait()
    mask_in.wait()
    low_half = lax.broadcasted_iota(jnp.int32, (OWN_R, 128), 1) < 64
    for t in range(NQ // 2):
        a = wig[:, t * 128:(t + 1) * 128].astype(F32)
        b = wig[:, 512 + t * 128:512 + (t + 1) * 128].astype(F32)
        wig_p[2 * t] = jnp.where(low_half, a, pltpu.roll(b, 64, 1)).astype(BF16)
        wig_p[2 * t + 1] = jnp.where(low_half, pltpu.roll(a, 64, 1), b).astype(BF16)

    b1_all = whole(b1, b1_s, b1_r, plane_peer(0, 1))
    b1_all.wait_recv()
    peak = stat[0:PT, :]
    for j in range(NQ - 1):
        peak = jnp.maximum(peak, b1[j, 0:PT, :])
    mass = stat[PT:2 * PT, :] * jnp.exp(stat[0:PT, :] - peak)
    for j in range(NQ - 1):
        mass = mass + b1[j, PT:2 * PT, :] * jnp.exp(b1[j, 0:PT, :] - peak)
    pair[...] = jnp.concatenate([peak, mass, blank], axis=0)
    pl.semaphore_wait(ring_known, 2)
    send(pair, b2, b2_s, b2_r, (p_id, (1 - zh) * NQ + q))

    for dx in far_first(NX):
        pl.semaphore_signal(known, inc=1, device_id=plane_peer(dx, 0), device_id_type=MESH)
    zs = [lax.rem(z + d, RING) for d in range(RING)]

    @pl.loop(0, PIX // 128)
    def _(j):
        span = pl.ds(pl.multiple_of(j * 128, 128), 128)
        pat_t[span, :] = pat[:, span].T

    b2_all = whole(b2, b2_s, b2_r, (p_id, (1 - zh) * NQ + q))
    b2_all.wait_recv()
    far_peak = b2[0:PT, :]
    top = jnp.maximum(peak, far_peak)
    mass = mass * jnp.exp(peak - top) + b2[PT:2 * PT, :] * jnp.exp(far_peak - top)
    part = jnp.zeros((8, OWN_R), F32)
    for t in range(PT):
        counts = mask[t * 128:(t + 1) * 128].astype(F32).reshape(1, 128)
        factor = counts / mass[t:t + 1, :]
        w = (jnp.exp(score[t] - top[t:t + 1, :]) * factor).T.astype(BF16)
        wt[t * 128:(t + 1) * 128, :] = w
        part = part + jnp.sum(w.astype(F32).reshape(16, 8, OWN_R), axis=0)
    occ1[...] = jnp.sum(part, axis=0, keepdims=True)

    pl.semaphore_wait(known, NX - 1)
    high_end = lax.div(zl, NZ // 2)
    for n in range(1, NZ):
        dz = high_end * n + (1 - high_end) * (NZ - n)
        for dx in (2, 1, 3, 0):
            peer = (xs[dx] * NZ + lax.rem(zl + dz, NZ), o_id)
            send(occ1, c1.at[dx * NZ + dz - 1], c1_s, c1_r, peer)
    for dx in far_first(NX):
        send(occ1, c1.at[dx * NZ - 1], c1_s, c1_r, pat_peer(dx, 0))

    def compress(i, carry):
        sums = []
        for n in range(4):
            first = n // 2 + 8 * (n % 2)
            rows = [
                pat_t[pl.ds(pl.multiple_of((16 * i + first + 2 * m) * ANGLES, ANGLES), ANGLES), :]
                for m in range(4)
            ]
            sums.append(dot(jnp.concatenate(rows, axis=0), wt[...]))
        evens = apply_table(fwd[0], sums[0], sums[2])
        odds = apply_table(fwd[1], sums[1], sums[3])
        one, two = (
            [v.reshape(ORD // 2, 8, OWN_R) for v in side] for side in (evens, odds)
        )
        cols = pl.ds(pl.multiple_of(i * 16, 16), 16)
        for par in range(2):
            whole_tile = jnp.concatenate(
                [jnp.where(upper, *((a, b) if par == 0 else (b, a))) for a, b in zip(one, two)],
                axis=1,
            )
            for h in range(NH):
                half = whole_tile[h * (ORD // 4):(h + 1) * (ORD // 4)]
                ordt[:, par, cols, h * OWN_R:(h + 1) * OWN_R] = half.astype(BF16)
        return carry

    lax.fori_loop(0, NBLK // 4, compress, 0)
    c1_all = whole(c1, c1_s, c1_r, pat_peer(1, 0))
    c1_all.wait_recv()
    sums = [occ1[...]] + [c1[j] for j in range(NX * NZ - 1)]
    while len(sums) > 1:
        sums = [a + b for a, b in zip(sums[::2], sums[1::2])]
    occ = sums[0]
    inv = (1.0 / math.sqrt(ORIENTS)) / (occ + 1.0)

    slot = lax.rem(lax.div(lax.broadcasted_iota(jnp.int32, (RADII, 128), 1), DEG), 4)

    inv_rows = jnp.broadcast_to(inv, (OWN_R, OWN_R)).T

    def project(i):
        g = qs[i]
        w = wig_p[g].astype(F32) * inv_rows
        both = jnp.concatenate([jnp.where(low_half, w, 0.0), jnp.where(low_half, 0.0, w)], axis=0)
        return dot(ordt[pl.ds(g * 2, 2)].reshape(BLK, 2 * OWN_R), both.astype(BF16))

    def share(i, out):
        g = qs[i]
        acc = [jnp.zeros((RADII, 128), F32)] * 2
        for kk in range(4):
            acc[kk % 2] = jnp.where(slot == kk, out[kk * RADII:(kk + 1) * RADII, :], acc[kk % 2])
        odd = pltpu.roll(acc[1].reshape(RADII // 8, 8, 128), 4, 1).reshape(RADII, 128)
        harm[g] = (acc[0] + odd).astype(BF16).reshape(NX, 16, 128)
        for dx in (2, 1, 3, 0):
            if dx or i:
                send(
                    harm.at[g, xs[dx]], e1.at[dx * NQ + i - 1], e1_s, e1_r,
                    plane_peer(dx, i),
                )

    order = far_first(NQ) + [0]
    ready = [project(order[0])]
    for n, i in enumerate(order):
        ready += [project(later) for later in order[len(ready):n + (3 if n else 2)]]
        share(i, ready[n])
    e1_all = whole(e1, e1_s, e1_r, plane_peer(1, 0))
    e1_all.wait_recv()
    tot = harm[q, x].astype(F32)
    sums = [tot] + [e1[j].astype(F32) for j in range(PLANE - 1)]
    while len(sums) > 1:
        sums = [a + b for a, b in zip(sums[::2], sums[1::2])]
    tot = sums[0]
    even, odd = tot[:8], tot[8:]
    first = lane[:8] < 64
    rows = jnp.concatenate(
        [
            jnp.where(first, even, pltpu.roll(odd, 64, 1)),
            jnp.where(first, pltpu.roll(even, 64, 1), odd),
        ],
        axis=0,
    )
    for j in range(RING):
        zsend[j] = rows[j:j + 1, :]
    for j in far_first(RING):
        send(zsend.at[zs[j]], e2.at[j - 1], e2_s, e2_r, ring_peer(j))
    e2_all = whole(e2, e2_s, e2_r, ring_peer(1))
    e2_all.wait_recv()
    fin = zsend[z]
    sums = [fin] + [e2[j] for j in range(RING - 1)]
    while len(sums) > 1:
        sums = [a + b for a, b in zip(sums[::2], sums[1::2])]
    fin = sums[0]
    out_ref[0:1, :] = fin[:, :64]
    out_ref[1:2, :] = fin[:, 64:]
    for copies in (b1_all, c1_all, e1_all, e2_all):
        copies.wait_send()
    pltpu.make_async_remote_copy(
        src_ref=pair, dst_ref=b2, send_sem=b2_s, recv_sem=b2_r,
        device_id=(p_id, (1 - zh) * NQ + q), device_id_type=MESH,
    ).wait_send()


def local(patterns, mask, model, wigner):
    syn, fwd = tables()
    hbm = pl.BlockSpec(memory_space=pltpu.MemorySpace.HBM)

    def in_hbm(value):
        return pltpu.with_memory_space_constraint(value, pltpu.MemorySpace.HBM)

    dma = pltpu.SemaphoreType.DMA
    out = pl.pallas_call(
        kernel,
        out_shape=jax.ShapeDtypeStruct((2, 64), F32),
        in_specs=[hbm] * 6,
        out_specs=pl.BlockSpec(memory_space=pltpu.VMEM),
        scratch_shapes=[
            pltpu.VMEM((OWN_P, PIX), BF16),
            pltpu.VMEM((OWN_P,), jnp.int32),
            pltpu.VMEM((RADII, HARM), F32),
            pltpu.VMEM((OWN_R, HARM), BF16),
            pltpu.VMEM(syn.shape, BF16),
            pltpu.VMEM(fwd.shape, BF16),
            pltpu.VMEM((PIX, OWN_P), BF16),
            pltpu.VMEM((NBLK, BLK, OWN_R), F32),
            pltpu.VMEM((PIX, OWN_R), BF16),
            pltpu.VMEM((PT, OWN_R, 128), F32),
            pltpu.VMEM((NQ, OWN_R, 128), BF16),
            pltpu.VMEM((OWN_P, OWN_R), BF16),
            pltpu.VMEM((ORD // 4, 2, RADII, 2 * OWN_R), BF16),
            pltpu.VMEM((8, 128), F32),
            pltpu.VMEM((NQ - 1, 8, 128), F32),
            pltpu.VMEM((8, 128), F32),
            pltpu.VMEM((8, 128), F32),
            pltpu.VMEM((1, 128), F32),
            pltpu.VMEM((NX * NZ - 1, 1, 128), F32),
            pltpu.VMEM((NQ, NX, 16, 128), BF16),
            pltpu.VMEM((PLANE - 1, 16, 128), BF16),
            pltpu.VMEM((RING, 1, 128), F32),
            pltpu.VMEM((RING - 1, 1, 128), F32),
        ]
        + [dma(())] * 16
        + [pltpu.SemaphoreType.REGULAR] * 2,
        compiler_params=pltpu.CompilerParams(
            collective_id=0, has_side_effects=True, vmem_limit_bytes=40 * 1024 * 1024
        ),
        name="recover",
    )(*(in_hbm(v) for v in (patterns, mask, model.T, wigner, jnp.asarray(syn), jnp.asarray(fwd))))
    return out.T


def solution(mesh):
    return jax.shard_map(
        local,
        mesh=mesh,
        in_specs=(P("pat", None), P("pat"), P(), P("ori", None)),
        out_specs=P("ori", "pat"),
        check_vma=False,
    )
```

```python
import math

import jax
import jax.numpy as jnp
import numpy as np
from jax import lax
from jax.experimental import pallas as pl
from jax.experimental.pallas import tpu as pltpu
from jax.sharding import PartitionSpec as P

RADII = 64
ANGLES = 64
DEG = 16
ORD = 64
PIX = 4096
HARM = 1024
PATTERNS = 12288
ORIENTS = 2048

TEMPER = 0.05
BACKGROUND = 0.1

NX, NZ = 4, 8
NH, NQ = 2, 8
PLANE = NX * NQ
RING = NH * NZ
OWN_P = PATTERNS // (NX * NZ)
OWN_R = ORIENTS // (NH * NQ)
PT = OWN_P // 128
BLK = 4 * ANGLES
NBLK = PIX // BLK

F32 = jnp.float32
BF16 = jnp.bfloat16
MESH = pl.DeviceIdType.MESH


def order_table():
    orders = np.arange(ORD)[:, None]
    angles = np.arange(ANGLES)[None, :]
    half = ANGLES // 2
    step = 2.0 * math.pi / ANGLES
    cos = np.cos(step * ((orders * angles) % ANGLES))
    sin = np.sin(step * (((orders - half) * angles) % ANGLES))
    return np.where(orders <= half, cos, sin).astype(np.float32)


def terms(full):
    high = full.astype(BF16)
    low = (full - high.astype(np.float32)).astype(BF16)
    return np.concatenate([high, high, low], axis=1)


def tables():
    table = order_table()
    eye = np.eye(4, dtype=np.float32)
    syn = np.einsum("ka,bc->bakc", table, eye).reshape(BLK, BLK)
    fwd = np.einsum("ka,bc->kbca", table * np.float32(2.0 / ANGLES), eye)
    swap = fwd[np.arange(ORD) ^ 1]
    return (
        terms(syn),
        np.stack([terms(fwd.reshape(BLK, BLK)), terms(swap.reshape(BLK, BLK))]),
    )


def split(value):
    high = value.astype(BF16)
    low = (value - high.astype(F32)).astype(BF16)
    return high, low


def dot(a, b):
    return jnp.dot(a, b, preferred_element_type=F32)


def apply_table(table, one, two):
    high, low = split(jnp.concatenate([one, two], axis=1))
    out = dot(table, jnp.concatenate([high, low, high], axis=0))
    return out[:, :OWN_R], out[:, OWN_R:]


def far_first(n):
    return sorted(range(1, n), key=lambda j: -min(j, n - j))


def kernel(
    pat_hbm, mask_hbm, model_hbm, wig_hbm, syn_hbm, fwd_hbm, out_ref,
    pat, mask, model, wig, syn, fwd,
    pat_t, cyc, logs, score, wig_p, wt, ordt,
    stat, b1, pair, b2, occ1, c1, harm, e1, zsend, e2,
    pat_sem, mask_sem, model_sem, wig_sem, syn_sem, fwd_sem,
    b1_s, b1_r, b2_s, b2_r, c1_s, c1_r, e1_s, e1_r, e2_s, e2_r, known, ring_known,
):
    p_id = lax.axis_index("pat")
    o_id = lax.axis_index("ori")
    x, zl = lax.div(p_id, NZ), lax.rem(p_id, NZ)
    zh, q = lax.div(o_id, NQ), lax.rem(o_id, NQ)
    z = zh * NZ + zl

    def plane_peer(dx, dq):
        return (xs[dx] * NZ + zl, zh * NQ + qs[dq])

    def ring_peer(dz):
        far = lax.rem(z + dz, RING)
        return (x * NZ + lax.rem(far, NZ), lax.div(far, NZ) * NQ + q)

    def pat_peer(dx, dz):
        return (xs[dx] * NZ + zls[dz], o_id)


    def greet(peer):
        pl.semaphore_signal(barrier, inc=1, device_id=peer, device_id_type=MESH)

    def send(src, dst, ssem, rsem, peer):
        pltpu.make_async_remote_copy(
            src_ref=src, dst_ref=dst, send_sem=ssem, recv_sem=rsem,
            device_id=peer, device_id_type=MESH,
        ).start()

    def whole(buf, ssem, rsem, peer):
        return pltpu.make_async_remote_copy(
            src_ref=buf, dst_ref=buf, send_sem=ssem, recv_sem=rsem,
            device_id=peer, device_id_type=MESH,
        )

    loads = [
        pltpu.make_async_copy(*refs)
        for refs in (
            (model_hbm, model, model_sem), (wig_hbm, wig, wig_sem), (syn_hbm, syn, syn_sem),
            (pat_hbm, pat, pat_sem), (fwd_hbm, fwd, fwd_sem), (mask_hbm, mask, mask_sem),
        )
    ]
    model_in, wig_in, syn_in, pat_in, fwd_in, mask_in = loads
    for load in loads:
        load.start()

    barrier = pltpu.get_barrier_semaphore()
    for d in (4, 12, 3, 13, 2, 14, 1, 15):
        greet(ring_peer(d))
    xs = [lax.rem(x + d, NX) for d in range(NX)]
    qs = [lax.rem(q + d, NQ) for d in range(NQ)]
    zls = [lax.rem(zl + d, NZ) for d in range(NZ)]
    for dx in far_first(NX):
        greet(plane_peer(dx, 0))
    for j in far_first(NQ):
        greet(plane_peer(0, j))

    row = lax.broadcasted_iota(jnp.int32, (16, 128), 0)
    lane = lax.broadcasted_iota(jnp.int32, (16, 128), 1)
    own = [
        jnp.where(lax.div(lane, DEG) == lax.div(row, 4) + n, 1.0, 0.0).astype(BF16)
        for n in (0, 4)
    ]
    upper = lax.broadcasted_iota(jnp.int32, (1, 8, 128), 1) < 4
    model_in.wait()
    wig_in.wait()

    def spread(value):
        tile = value.reshape(RADII // 8, 8, 128)
        other = pltpu.roll(tile, 4, 1)
        one = jnp.where(upper, tile, other)
        two = jnp.where(upper, other, tile)
        rows = []
        for i in range(RADII // 8):
            for half in (one[i], two[i]):
                packed = jnp.concatenate([half, half], axis=0).astype(BF16)
                rows += [packed * own[0], packed * own[1]]
        return jnp.concatenate(rows, axis=0)

    def gather_cycles(g):
        cols = pl.ds(pl.multiple_of(g * 128, 128), 128)
        m = model[:, cols]
        high = m.astype(BF16).astype(F32)
        left = jnp.concatenate([spread(high), spread(m - high)], axis=1)
        w = wig[:, cols]
        out = lax.dot_general(
            left, jnp.concatenate([w, w], axis=1), (((1,), (1,)), ((), ())),
            preferred_element_type=F32,
        )
        cyc[:, pl.ds(pl.multiple_of(g * 32, 32), 32), :] = out.reshape(NBLK, 32, OWN_R)

    for g in range(ORD // 8):
        gather_cycles(g)

    syn_in.wait()

    def expand(h, total):
        for m in range(0, NBLK // 2, 2):
            j = h * (NBLK // 2) + m
            for n, part in enumerate(apply_table(syn[...], cyc[j], cyc[j + 1])):
                value = (BACKGROUND + part).astype(BF16)
                logs[pl.ds(pl.multiple_of((j + n) * BLK, BLK), BLK), :] = value
                e = jnp.exp(value.astype(F32))
                total = total + jnp.sum(e.reshape(BLK // 8, 8, OWN_R), axis=0)
        return total

    total = lax.fori_loop(0, 2, expand, jnp.zeros((8, OWN_R), F32))
    intensity = jnp.sum(total, axis=0, keepdims=True)

    pl.semaphore_wait(barrier, 8 + NX - 1 + NQ - 1)
    for d in (4, 12):
        pl.semaphore_signal(ring_known, inc=1, device_id=ring_peer(d), device_id_type=MESH)

    pat_in.wait()
    scaled = TEMPER * (dot(pat[...], logs[...]) - intensity)
    for t in range(PT):
        score[t] = scaled[t * 128:(t + 1) * 128, :].T
    peaks, masses = [], []
    for t in range(PT):
        s = score[t]
        m = jnp.max(s, axis=0, keepdims=True)
        peaks.append(m)
        masses.append(jnp.sum(jnp.exp(s - m), axis=0, keepdims=True))
    blank = jnp.zeros((8 - 2 * PT, 128), F32)
    stat[...] = jnp.concatenate(peaks + masses + [blank], axis=0)

    for j in far_first(NQ):
        send(stat, b1.at[j - 1], b1_s, b1_r, plane_peer(0, j))

    fwd_in.wait()
    mask_in.wait()
    low_half = lax.broadcasted_iota(jnp.int32, (OWN_R, 128), 1) < 64
    for t in range(NQ // 2):
        a = wig[:, t * 128:(t + 1) * 128].astype(F32)
        b = wig[:, 512 + t * 128:512 + (t + 1) * 128].astype(F32)
        wig_p[2 * t] = jnp.where(low_half, a, pltpu.roll(b, 64, 1)).astype(BF16)
        wig_p[2 * t + 1] = jnp.where(low_half, pltpu.roll(a, 64, 1), b).astype(BF16)

    b1_all = whole(b1, b1_s, b1_r, plane_peer(0, 1))
    b1_all.wait_recv()
    peak = stat[0:PT, :]
    for j in range(NQ - 1):
        peak = jnp.maximum(peak, b1[j, 0:PT, :])
    mass = stat[PT:2 * PT, :] * jnp.exp(stat[0:PT, :] - peak)
    for j in range(NQ - 1):
        mass = mass + b1[j, PT:2 * PT, :] * jnp.exp(b1[j, 0:PT, :] - peak)
    pair[...] = jnp.concatenate([peak, mass, blank], axis=0)
    pl.semaphore_wait(ring_known, 2)
    send(pair, b2, b2_s, b2_r, (p_id, (1 - zh) * NQ + q))

    for dx in far_first(NX):
        pl.semaphore_signal(known, inc=1, device_id=plane_peer(dx, 0), device_id_type=MESH)
    zs = [lax.rem(z + d, RING) for d in range(RING)]

    @pl.loop(0, PIX // 128)
    def _(j):
        span = pl.ds(pl.multiple_of(j * 128, 128), 128)
        pat_t[span, :] = pat[:, span].T

    b2_all = whole(b2, b2_s, b2_r, (p_id, (1 - zh) * NQ + q))
    b2_all.wait_recv()
    far_peak = b2[0:PT, :]
    top = jnp.maximum(peak, far_peak)
    mass = mass * jnp.exp(peak - top) + b2[PT:2 * PT, :] * jnp.exp(far_peak - top)
    part = jnp.zeros((8, OWN_R), F32)
    for t in range(PT):
        counts = mask[t * 128:(t + 1) * 128].astype(F32).reshape(1, 128)
        factor = counts / mass[t:t + 1, :]
        w = (jnp.exp(score[t] - top[t:t + 1, :]) * factor).T.astype(BF16)
        wt[t * 128:(t + 1) * 128, :] = w
        part = part + jnp.sum(w.astype(F32).reshape(16, 8, OWN_R), axis=0)
    occ1[...] = jnp.sum(part, axis=0, keepdims=True)

    pl.semaphore_wait(known, NX - 1)
    high_end = lax.div(zl, NZ // 2)
    for n in range(1, NZ):
        dz = high_end * n + (1 - high_end) * (NZ - n)
        for dx in (2, 1, 3, 0):
            peer = (xs[dx] * NZ + lax.rem(zl + dz, NZ), o_id)
            send(occ1, c1.at[dx * NZ + dz - 1], c1_s, c1_r, peer)
    for dx in far_first(NX):
        send(occ1, c1.at[dx * NZ - 1], c1_s, c1_r, pat_peer(dx, 0))

    def compress(i, carry):
        sums = []
        for n in range(4):
            first = n // 2 + 8 * (n % 2)
            rows = [
                pat_t[pl.ds(pl.multiple_of((16 * i + first + 2 * m) * ANGLES, ANGLES), ANGLES), :]
                for m in range(4)
            ]
            sums.append(dot(jnp.concatenate(rows, axis=0), wt[...]))
        evens = apply_table(fwd[0], sums[0], sums[2])
        odds = apply_table(fwd[1], sums[1], sums[3])
        one, two = (
            [v.reshape(ORD // 2, 8, OWN_R) for v in side] for side in (evens, odds)
        )
        cols = pl.ds(pl.multiple_of(i * 16, 16), 16)
        for par in range(2):
            whole_tile = jnp.concatenate(
                [jnp.where(upper, *((a, b) if par == 0 else (b, a))) for a, b in zip(one, two)],
                axis=1,
            )
            for h in range(NH):
                half = whole_tile[h * (ORD // 4):(h + 1) * (ORD // 4)]
                ordt[:, par, cols, h * OWN_R:(h + 1) * OWN_R] = half.astype(BF16)
        return carry

    lax.fori_loop(0, NBLK // 4, compress, 0)
    c1_all = whole(c1, c1_s, c1_r, pat_peer(1, 0))
    c1_all.wait_recv()
    sums = [occ1[...]] + [c1[j] for j in range(NX * NZ - 1)]
    while len(sums) > 1:
        sums = [a + b for a, b in zip(sums[::2], sums[1::2])]
    occ = sums[0]
    inv = (1.0 / math.sqrt(ORIENTS)) / (occ + 1.0)

    slot = lax.rem(lax.div(lax.broadcasted_iota(jnp.int32, (RADII, 128), 1), DEG), 4)

    inv_rows = jnp.broadcast_to(inv, (OWN_R, OWN_R)).T

    def project(i):
        g = qs[i]
        w = wig_p[g].astype(F32) * inv_rows
        both = jnp.concatenate([jnp.where(low_half, w, 0.0), jnp.where(low_half, 0.0, w)], axis=0)
        return dot(ordt[pl.ds(g * 2, 2)].reshape(BLK, 2 * OWN_R), both.astype(BF16))

    def share(i, out):
        g = qs[i]
        acc = [jnp.zeros((RADII, 128), F32)] * 2
        for kk in range(4):
            acc[kk % 2] = jnp.where(slot == kk, out[kk * RADII:(kk + 1) * RADII, :], acc[kk % 2])
        odd = pltpu.roll(acc[1].reshape(RADII // 8, 8, 128), 4, 1).reshape(RADII, 128)
        harm[g] = (acc[0] + odd).astype(BF16).reshape(NX, 16, 128)
        for dx in (2, 1, 3, 0):
            if dx or i:
                send(
                    harm.at[g, xs[dx]], e1.at[dx * NQ + i - 1], e1_s, e1_r,
                    plane_peer(dx, i),
                )

    order = far_first(NQ) + [0]
    ready = [project(order[0])]
    for n, i in enumerate(order):
        ready += [project(later) for later in order[len(ready):n + (3 if n else 1)]]
        share(i, ready[n])
    e1_all = whole(e1, e1_s, e1_r, plane_peer(1, 0))
    e1_all.wait_recv()
    tot = harm[q, x].astype(F32)
    sums = [tot] + [e1[j].astype(F32) for j in range(PLANE - 1)]
    while len(sums) > 1:
        sums = [a + b for a, b in zip(sums[::2], sums[1::2])]
    tot = sums[0]
    even, odd = tot[:8], tot[8:]
    first = lane[:8] < 64
    rows = jnp.concatenate(
        [
            jnp.where(first, even, pltpu.roll(odd, 64, 1)),
            jnp.where(first, pltpu.roll(even, 64, 1), odd),
        ],
        axis=0,
    )
    for j in range(RING):
        zsend[j] = rows[j:j + 1, :]
    for j in far_first(RING):
        send(zsend.at[zs[j]], e2.at[j - 1], e2_s, e2_r, ring_peer(j))
    e2_all = whole(e2, e2_s, e2_r, ring_peer(1))
    e2_all.wait_recv()
    fin = zsend[z]
    sums = [fin] + [e2[j] for j in range(RING - 1)]
    while len(sums) > 1:
        sums = [a + b for a, b in zip(sums[::2], sums[1::2])]
    fin = sums[0]
    out_ref[0:1, :] = fin[:, :64]
    out_ref[1:2, :] = fin[:, 64:]
    for copies in (b1_all, c1_all, e1_all, e2_all):
        copies.wait_send()
    pltpu.make_async_remote_copy(
        src_ref=pair, dst_ref=b2, send_sem=b2_s, recv_sem=b2_r,
        device_id=(p_id, (1 - zh) * NQ + q), device_id_type=MESH,
    ).wait_send()


def local(patterns, mask, model, wigner):
    syn, fwd = tables()
    hbm = pl.BlockSpec(memory_space=pltpu.MemorySpace.HBM)

    def in_hbm(value):
        return pltpu.with_memory_space_constraint(value, pltpu.MemorySpace.HBM)

    dma = pltpu.SemaphoreType.DMA
    out = pl.pallas_call(
        kernel,
        out_shape=jax.ShapeDtypeStruct((2, 64), F32),
        in_specs=[hbm] * 6,
        out_specs=pl.BlockSpec(memory_space=pltpu.VMEM),
        scratch_shapes=[
            pltpu.VMEM((OWN_P, PIX), BF16),
            pltpu.VMEM((OWN_P,), jnp.int32),
            pltpu.VMEM((RADII, HARM), F32),
            pltpu.VMEM((OWN_R, HARM), BF16),
            pltpu.VMEM(syn.shape, BF16),
            pltpu.VMEM(fwd.shape, BF16),
            pltpu.VMEM((PIX, OWN_P), BF16),
            pltpu.VMEM((NBLK, BLK, OWN_R), F32),
            pltpu.VMEM((PIX, OWN_R), BF16),
            pltpu.VMEM((PT, OWN_R, 128), F32),
            pltpu.VMEM((NQ, OWN_R, 128), BF16),
            pltpu.VMEM((OWN_P, OWN_R), BF16),
            pltpu.VMEM((ORD // 4, 2, RADII, 2 * OWN_R), BF16),
            pltpu.VMEM((8, 128), F32),
            pltpu.VMEM((NQ - 1, 8, 128), F32),
            pltpu.VMEM((8, 128), F32),
            pltpu.VMEM((8, 128), F32),
            pltpu.VMEM((1, 128), F32),
            pltpu.VMEM((NX * NZ - 1, 1, 128), F32),
            pltpu.VMEM((NQ, NX, 16, 128), BF16),
            pltpu.VMEM((PLANE - 1, 16, 128), BF16),
            pltpu.VMEM((RING, 1, 128), F32),
            pltpu.VMEM((RING - 1, 1, 128), F32),
        ]
        + [dma(())] * 16
        + [pltpu.SemaphoreType.REGULAR] * 2,
        compiler_params=pltpu.CompilerParams(
            collective_id=0, has_side_effects=True, vmem_limit_bytes=40 * 1024 * 1024
        ),
        name="recover",
    )(*(in_hbm(v) for v in (patterns, mask, model.T, wigner, jnp.asarray(syn), jnp.asarray(fwd))))
    return out.T


def solution(mesh):
    return jax.shard_map(
        local,
        mesh=mesh,
        in_specs=(P("pat", None), P("pat"), P(), P("ori", None)),
        out_specs=P("ori", "pat"),
        check_vma=False,
    )
```
